32 devices in a mesh: row: 16 (over z, x, core), col: 2 (over y).
Axes of the slice: x: 2, y: 2, z: 4, core: 2. Of those that a mesh axis runs over, the one named last changes fastest.
Arguments:
- template: float32 [32, 16, 2048], P(None, 'row', 'col'), may hold values from -6 to 6
- target: float32 [32, 16, 2048], P(None, 'row', 'col'), may hold values from -6 to 6
- velocity: float32 [3, 32, 16, 2048], P(None, None, 'row', 'col'), may hold values from -0.6 to 0.6
- departure: int32 [32, 1, 2048], P('row', None, 'col'), may hold values from -48 to 48
- weights: float32 [8, 4], replicated, may hold values from -0.1 to 1, as said below
Outputs:
- gradient: float32 [3, 32, 16, 2048], P(None, 'row', 'col')
The draws below stay inside these ranges and needn't reach their ends.
Inputs may be any that keep to these rules, and one draw needn't show every extreme that they name: Row q holds the four weights of a cubic interpolation at a fraction between q / 8 and (q + 1) / 8; each row sums to one.
All inputs are finite; a program needn't handle non-finite values.
Results may differ from the reference program's by a relative error of at most 0.0001.
Values sent between devices are 32-bit elements; how exact they have to be, the bound alone decides.
A program may use at most 64 MiB of HBM per device.

```python
import math
import jax
import jax.numpy as jnp

NZ = 2048
LB = 16
QUANT = 8
SHIFT = 6
TAPS = 4
NX = 32
NY = 16


def draw_weights(key, part):
    levels = jnp.arange(QUANT, dtype=jnp.float32)[:, None]
    spread = jax.random.uniform(key, (QUANT, 1), jnp.float32)
    point = (levels + spread) / QUANT
    tap_first = -point * (point - 1.0) * (point - 2.0) / 6.0
    tap_second = (point + 1.0) * (point - 1.0) * (point - 2.0) / 2.0
    tap_third = -(point + 1.0) * point * (point - 2.0) / 2.0
    tap_fourth = (point + 1.0) * point * (point - 1.0) / 6.0
    return jnp.concatenate([tap_first, tap_second, tap_third, tap_fourth], axis=1)


def with_ends(values, own_key, least, largest):
    dims = values.shape
    index_at = [jax.random.randint(jax.random.fold_in(own_key, axis), (), 0, dims[axis]) for axis in range(len(dims))]
    values = values.at[tuple(index_at)].set(least)
    longest = dims.index(max(dims))
    index_at[longest] = (index_at[longest] + 1) % dims[longest]
    return values.at[tuple(index_at)].set(largest)


def shard_levels(own_key, extent, pieces, low, largest):
    gain = 1.0
    for position, blocks in pieces:
        draws = jax.random.uniform(jax.random.fold_in(jax.random.fold_in(own_key, 6), position), (blocks,), jnp.float32, low / len(pieces), largest / len(pieces))
        gain = gain * jnp.repeat(jnp.exp(draws), extent[position] // blocks).reshape((-1,) + (1,) * (len(extent) - 1 - position))
    return gain


def normal_values(stream_key, dims, scale, most, pieces=(), kind=jnp.bfloat16):
    array = jax.random.normal(stream_key, dims, jnp.float32) * scale
    if len(pieces) > 0:
        array = shard_levels(stream_key, dims, pieces, -0.22, 0.18) * array
    return jnp.clip(array, min=-most, max=most).astype(kind)


def setup_inputs(seed: int = 0) -> dict:
    splits = jax.random.split(jax.random.key(seed), 6)
    template = normal_values(splits[0], (NX, NY, NZ), 1.0, 6.0, ((1, 16), (2, 2)), jnp.float32)
    target = normal_values(splits[1], (NX, NY, NZ), 1.0, 6.0, ((1, 16), (2, 2)), jnp.float32)
    velocity = normal_values(splits[2], (3, NX, NY, NZ), 0.1, 0.6, ((2, 16), (3, 2)), jnp.float32)
    departure = with_ends(jax.random.randint(splits[3], (NX, NY // LB, NZ), -SHIFT * QUANT, SHIFT * QUANT + 1), jax.random.fold_in(splits[3], 1), -SHIFT * QUANT, SHIFT * QUANT).astype(jnp.int32)
    weights = draw_weights(jax.random.fold_in(splits[5], 71), 0)
    return dict(template=template, target=target, velocity=velocity, departure=departure, weights=weights)


BETA = 0.5


def central(values, axis):
    return (jnp.roll(values, -1, axis) - jnp.roll(values, 1, axis)) * 0.5


def second_difference(values, axis):
    return 2.0 * values - jnp.roll(values, -1, axis) - jnp.roll(values, 1, axis)


def reference(template, target, velocity, departure, weights):
    shift_cells = jnp.floor_divide(departure, QUANT).astype(jnp.int32)
    levels = (departure - shift_cells * QUANT).astype(jnp.int32)
    shift_cells = jnp.repeat(shift_cells, LB, axis=1)
    levels = jnp.repeat(levels, LB, axis=1)
    lines = template.shape[1]
    line_index = jnp.arange(lines, dtype=jnp.int32)[None, :, None]
    moved_image = jnp.zeros(template.shape, jnp.float32)
    for tap in range(TAPS):
        source_index = jnp.mod(line_index - shift_cells - 1 + tap, lines).astype(jnp.int32)
        moved_image = moved_image + weights[levels, tap] * jnp.take_along_axis(template, source_index, axis=1)
    misfit = target - moved_image
    frequency = jnp.fft.fftfreq(NZ) * NZ
    symbol = ((2.0 * math.pi / NZ) * frequency) ** 2
    components = []
    for comp_index in range(3):
        component = velocity[comp_index]
        second = second_difference(component, 0) + second_difference(component, 1)
        spectrum = jnp.fft.fft(component, axis=2)
        bending = jnp.real(jnp.fft.ifft(spectrum * symbol, axis=2)).astype(jnp.float32)
        force = misfit * central(moved_image, comp_index)
        components.append(BETA * (second + bending) + force)
    return jnp.stack(components)
```

```python
import functools
import math

import jax
import jax.numpy as jnp
import numpy as np
from jax import lax
from jax.experimental import pallas as pl
from jax.experimental.pallas import tpu as pltpu
from jax.sharding import PartitionSpec as P

QUANT = 8
TAPS = 4


BETA = 0.5
HIGH = lax.Precision.HIGHEST
LANES = 128
SUBLANES = 8
MESH = pl.DeviceIdType.MESH


def with_halo(block, sides, width):
    for axis, dim in sides:
        count = lax.axis_size(axis)
        forward = [(i, i + 1) for i in range(count - 1)]
        forward.append((count - 1, 0))
        backward = [(target, source) for source, target in forward]
        low = lax.ppermute(
            lax.slice_in_dim(block, block.shape[dim] - width, None, axis=dim), axis, forward
        )
        high = lax.ppermute(lax.slice_in_dim(block, 0, width, axis=dim), axis, backward)
        block = jnp.concatenate([low, block, high], axis=dim)
    return block


def central(values, axis):
    return (jnp.roll(values, -1, axis) - jnp.roll(values, 1, axis)) * 0.5


def second_difference(values, axis):
    return 2.0 * values - jnp.roll(values, -1, axis) - jnp.roll(values, 1, axis)


def tap_weights(levels, weight):
    taps = []
    for tap in range(TAPS):
        value = jnp.zeros(levels.shape, jnp.float32)
        for level in range(QUANT):
            value = jnp.where(levels == level, weight(level, tap), value)
        taps.append(value)
    return taps


def transport(template_y, departure, weights):
    planes, lines, columns = template_y.shape
    blocks = departure.shape[1]
    span = lines // blocks
    shift_cells = jnp.floor_divide(departure, QUANT)
    levels = departure - shift_cells * QUANT
    taps = tap_weights(levels, lambda level, tap: weights[level, tap])
    shift = jnp.mod(shift_cells + 1, lines)
    parts = []
    for block in range(blocks):
        rolled = template_y
        step = 1
        while step < lines:
            chosen = (shift[:, block : block + 1] & step) != 0
            rolled = jnp.where(chosen, jnp.roll(rolled, step, 1), rolled)
            step *= 2
        part = 0.0
        for tap in range(TAPS):
            turned = jnp.roll(rolled, -tap - block * span, 1)[:, :span]
            part = part + taps[tap][:, block : block + 1] * turned
        parts.append(part)
    return jnp.concatenate(parts, axis=1)


def curvature(velocity_z):
    field_shape = velocity_z.shape
    length = field_shape[-1]
    inner = 128
    outer = length // inner
    lines = velocity_z.reshape(-1, outer, inner)
    angle = 2.0 * math.pi / length
    outer_index = jnp.arange(outer, dtype=jnp.int32)
    inner_index = jnp.arange(inner, dtype=jnp.int32)
    outer_phase = (
        jnp.mod(outer_index[:, None] * outer_index[None, :] * inner, length).astype(jnp.float32)
        * angle
    )
    cos_outer = jnp.cos(outer_phase)
    sin_outer = jnp.sin(outer_phase)
    twist_phase = (
        jnp.mod(outer_index[:, None] * inner_index[None, :], length).astype(jnp.float32) * angle
    )
    cos_twist = jnp.cos(twist_phase)
    sin_twist = jnp.sin(twist_phase)
    inner_phase = (
        jnp.mod(inner_index[:, None] * inner_index[None, :] * outer, length).astype(jnp.float32)
        * angle
    )
    cos_inner = jnp.cos(inner_phase)
    sin_inner = jnp.sin(inner_phase)
    freq_index = outer_index[:, None] + outer * inner_index[None, :]
    signed = jnp.where(freq_index < length // 2, freq_index, freq_index - length).astype(
        jnp.float32
    )
    symbol = (signed * angle) ** 2 / length
    real_one = jnp.einsum("lap,ak->lkp", lines, cos_outer, precision=HIGH)
    imag_one = -jnp.einsum("lap,ak->lkp", lines, sin_outer, precision=HIGH)
    real_two = real_one * cos_twist + imag_one * sin_twist
    imag_two = imag_one * cos_twist - real_one * sin_twist
    real_three = jnp.einsum("lkp,pq->lkq", real_two, cos_inner, precision=HIGH) + jnp.einsum(
        "lkp,pq->lkq", imag_two, sin_inner, precision=HIGH
    )
    imag_three = jnp.einsum("lkp,pq->lkq", imag_two, cos_inner, precision=HIGH) - jnp.einsum(
        "lkp,pq->lkq", real_two, sin_inner, precision=HIGH
    )
    real_three = real_three * symbol
    imag_three = imag_three * symbol
    real_four = jnp.einsum("lkq,pq->lkp", real_three, cos_inner, precision=HIGH) - jnp.einsum(
        "lkq,pq->lkp", imag_three, sin_inner, precision=HIGH
    )
    imag_four = jnp.einsum("lkq,pq->lkp", imag_three, cos_inner, precision=HIGH) + jnp.einsum(
        "lkq,pq->lkp", real_three, sin_inner, precision=HIGH
    )
    real_five = real_four * cos_twist - imag_four * sin_twist
    imag_five = imag_four * cos_twist + real_four * sin_twist
    result = jnp.einsum("lkp,kn->lnp", real_five, cos_outer, precision=HIGH) - jnp.einsum(
        "lkp,kn->lnp", imag_five, sin_outer, precision=HIGH
    )
    return result.reshape(field_shape)


def spectral(arrived):
    return (arrived, curvature(arrived[3:6]))


def per_device(template, target, velocity, departure, weights):
    across = second_difference(velocity, 1)
    bundle = jnp.concatenate([template[None], target[None], velocity, across], axis=0)
    regrouped = lax.all_to_all(bundle, "row", split_axis=1, concat_axis=2, tiled=True)
    moved_image = transport(regrouped[0], departure, weights)
    misfit = regrouped[1] - moved_image
    pull_along = misfit * central(moved_image, 1)
    velocity_y = regrouped[2:5]
    second_part = second_difference(velocity_y, 2)
    second_part = regrouped[5:8] + second_part
    outgoing = jnp.concatenate(
        [misfit[None], moved_image[None], pull_along[None], velocity_y, second_part], axis=0
    )
    columns_z, bending = spectral(
        lax.all_to_all(outgoing, "col", split_axis=2, concat_axis=3, tiled=True)
    )
    misfit_z = columns_z[0]
    moved_z = columns_z[1]
    second_z = columns_z[6:9]
    padded = with_halo(moved_z, (("row", 0),), 1)
    slope_across = (padded[2:] - padded[:-2]) * 0.5
    force = jnp.stack([misfit_z * slope_across, columns_z[2], misfit_z * central(moved_z, 2)])
    return BETA * (second_z + bending) + force


def split_halves(values):
    high = values.astype(jnp.bfloat16)
    return high, (values - high.astype(jnp.float32)).astype(jnp.bfloat16)


def dot_split(left, right):
    dot = functools.partial(jnp.dot, preferred_element_type=jnp.float32)
    return dot(left[0], right[0]) + (dot(left[0], right[1]) + dot(left[1], right[0]))


def halves_of(matrix):
    high = matrix.astype(np.float32).astype(jnp.bfloat16)
    low = (matrix - high.astype(np.float64)).astype(np.float32).astype(jnp.bfloat16)
    return np.stack([high, low])


def operators(length, rows):
    outer = length // LANES
    frequency = np.fft.fftfreq(length) * length
    response = np.real(np.fft.ifft((2.0 * math.pi / length * frequency) ** 2))
    response[0] += 4.0
    response *= BETA
    inner = np.arange(LANES)
    group = np.arange(outer)
    away = np.mod(
        LANES * group[:, None, None] + inner[None, :, None] - inner[None, None, :], length
    )
    mixed = np.fft.fft(response[away], axis=0)
    pairs = []
    forward = np.zeros((outer, outer))
    inverse = np.zeros((outer, outer))
    forward[0] = 1.0
    forward[1] = (-1.0) ** group
    inverse[:, 0] = 1.0 / outer
    inverse[:, 1] = (-1.0) ** group / outer
    zero = np.zeros((LANES, LANES))
    pairs.append(np.block([[mixed[0].real.T, zero], [zero, mixed[outer // 2].real.T]]))
    for k in range(1, outer // 2):
        real, imag = mixed[k].real.T, mixed[k].imag.T
        pairs.append(np.block([[real, imag], [-imag, real]]))
        phase = 2.0 * math.pi * k * group / outer
        forward[2 * k] = np.cos(phase)
        forward[2 * k + 1] = -np.sin(phase)
        inverse[:, 2 * k] = 2.0 * np.cos(phase) / outer
        inverse[:, 2 * k + 1] = -2.0 * np.sin(phase) / outer
    same = np.eye(rows)
    ahead = np.kron(forward, same)
    back = np.kron(inverse, same)
    return halves_of(ahead), halves_of(np.stack(pairs)), halves_of(back)


def kernel(
    extent,
    template,
    target,
    velocity,
    departure,
    weights,
    ahead_hbm,
    pairs_hbm,
    back_hbm,
    out,
    template_y,
    target_z,
    velocity_z,
    edge,
    extended,
    extended_edge,
    moved,
    moved_edge,
    moved_low,
    moved_high,
    slope,
    rest,
    spectrum,
    ahead,
    pairs,
    back,
    load_sem,
    send_sem,
    recv_sem,
):
    rows, columns = extent
    row, column = lax.axis_index("row"), lax.axis_index("col")
    planes, lines, slab = template_y.shape[:3]
    components = velocity_z.shape[0]
    own = lines // columns
    outer = columns * slab
    owner = row // own
    place = lax.rem(row, own)
    groups = [pl.ds(0, components - 1), pl.ds(components - 1, 1)]
    TEMPLATE, TARGET, MOVED, MOVED_EDGE, LOW, HIGH_SIDE, VELOCITY = 0, 1, 2, 3, 5, 6, 7
    SIDE_LOW, SIDE_HIGH, EDGE_LOW, EDGE_HIGH = (
        VELOCITY + i * len(groups) for i in range(1, 5)
    )
    extent_x = velocity.shape[1]
    here_z = pl.ds(pl.multiple_of(column * slab, slab), slab)

    loads = [
        pltpu.make_async_copy(source, sink, load_sem.at[i])
        for i, (source, sink) in enumerate(
            [(ahead_hbm, ahead), (pairs_hbm, pairs), (back_hbm, back)]
        )
    ]

    barrier = pltpu.get_barrier_semaphore()
    for i in range(rows):
        for j in range(columns):
            if i + j > 0:
                pl.semaphore_signal(
                    barrier,
                    inc=1,
                    device_id=(lax.rem(row + i, rows), lax.rem(column + j, columns)),
                    device_id_type=MESH,
                )
    for load in loads:
        load.start()
    pl.semaphore_wait(barrier, rows * columns - 1)

    def remote(source, sink, kind, to):
        return pltpu.make_async_remote_copy(
            src_ref=source,
            dst_ref=sink,
            send_sem=send_sem.at[kind],
            recv_sem=recv_sem.at[kind],
            device_id=to,
            device_id_type=MESH,
        )

    pending = []

    def deliver(source, sink, kind, to, near=None):
        if near is None:
            remote(source, sink, kind, to).start()
        else:

            @pl.when(near)
            def _():
                pltpu.make_async_copy(source, sink, recv_sem.at[kind]).start()

            @pl.when(jnp.logical_not(near))
            def _():
                remote(source, sink, kind, to).start()

        pending.append((near, source, sink, kind, to))

    def arrived(ref, kind):
        pltpu.make_async_copy(ref, ref, recv_sem.at[kind]).wait()

    inside = owner == column
    others = []
    for d in [*range(1, columns), 0]:
        for i in range(own):
            others.append(
                (d + i == 0, lax.rem(owner + d, columns) * own + lax.rem(place + i, own))
            )

    def send_template():
        for mine, to in others:
            source = template.at[pl.ds(to * planes, planes)]
            sink = template_y.at[:, row]
            if mine:
                pltpu.make_async_copy(source, sink, recv_sem.at[TEMPLATE]).start()
            else:
                deliver(source, sink, TEMPLATE, (to, column))

    def send_target():
        for mine, to in others:
            deliver(
                target.at[pl.ds(to * planes, planes)],
                target_z.at[:, here_z, place],
                TARGET,
                (to, owner),
                inside if mine else None,
            )

    def send_velocity(group):
        comps = groups[group]
        for h in range(columns):
            for to, plane, at in (
                (h * own, (h * own * planes - 1) % extent_x, 0),
                (h * own + own - 1, (h + 1) * own * planes % extent_x, planes + 1),
            ):
                deliver(
                    velocity.at[comps, plane],
                    velocity_z.at[comps, at, here_z, place],
                    VELOCITY + group,
                    (to, owner),
                    jnp.logical_and(inside, row == to),
                )
        for mine, to in others:
            deliver(
                velocity.at[comps, pl.ds(to * planes, planes)],
                velocity_z.at[comps, pl.ds(1, planes), here_z, place],
                VELOCITY + group,
                (to, owner),
                inside if mine else None,
            )

    def send_beside(group, start):
        comps = groups[group]
        mine = pl.ds(1, planes)

        def go(*copy):
            if start:
                remote(*copy).start()
            else:
                remote(*copy).wait_send()

        go(
            velocity_z.at[comps, mine, :, own - 1],
            edge.at[comps, :, :, 0],
            EDGE_LOW + group,
            (row, lax.rem(column + 1, columns)),
        )
        go(
            velocity_z.at[comps, mine, :, 0],
            edge.at[comps, :, :, 1],
            EDGE_HIGH + group,
            (row, lax.rem(column + columns - 1, columns)),
        )

        @pl.when(place < own - 1)
        def _():
            go(
                velocity_z.at[comps, planes],
                velocity_z.at[comps, 0],
                SIDE_LOW + group,
                (lax.rem(row + 1, rows), column),
            )

        @pl.when(place > 0)
        def _():
            go(
                velocity_z.at[comps, 1],
                velocity_z.at[comps, planes + 1],
                SIDE_HIGH + group,
                (lax.rem(row + rows - 1, rows), column),
            )

    def transport_lines():
        blocks = departure.shape[1]
        span = lines // blocks
        for plane in range(planes):
            image = [template_y[plane, y] for y in range(lines)]
            values = []
            for block in range(blocks):
                offset = departure[plane, block]
                whole = offset >> (QUANT.bit_length() - 1)
                levels = offset - whole * QUANT
                taps = tap_weights(levels, lambda level, tap: weights[tap, level])
                shift = jnp.where(whole + 1 < 0, whole + 1 + lines, whole + 1)
                rolled = image
                step = 1
                while step < lines:
                    chosen = (shift & step) != 0
                    rolled = [
                        jnp.where(chosen, rolled[(y - step) % lines], rolled[y])
                        for y in range(lines)
                    ]
                    step *= 2
                for y in range(block * span, (block + 1) * span):
                    value = taps[0] * rolled[y]
                    for tap in range(1, TAPS):
                        value = value + taps[tap] * rolled[(y + tap) % lines]
                    values.append(value)
            for y in range(lines):
                extended[plane, y // own, :, y % own, :] = values[y]
            for j in range(columns):
                extended_edge[plane, j, :, 0, :] = values[(j * own - 1) % lines]
                extended_edge[plane, j, :, 1, :] = values[(j * own + own) % lines]

    def send_moved():
        up, down = lax.rem(row + 1, rows), lax.rem(row + rows - 1, rows)
        for j in range(columns):
            to = lax.rem(column + j, columns)
            deliver(extended.at[planes - 1, to], moved_low.at[here_z], LOW, (up, to))
            deliver(extended.at[0, to], moved_high.at[here_z], HIGH_SIDE, (down, to))
            if j > 0:
                deliver(extended.at[:, to], moved.at[:, here_z], MOVED, (row, to))
                for r in range(2):
                    deliver(
                        extended_edge.at[:, to, :, r],
                        moved_edge.at[:, here_z, r],
                        MOVED_EDGE + r,
                        (row, to),
                    )
        moved[:, here_z] = extended[:, column]
        moved_edge[:, here_z] = extended_edge[:, column]

    def velocity_arrived(group):
        comps = groups[group]

        @pl.when(place == 0)
        def _():
            arrived(velocity_z.at[comps, pl.ds(0, planes + 1)], VELOCITY + group)

        @pl.when(place == own - 1)
        def _():
            arrived(velocity_z.at[comps, pl.ds(1, planes + 1)], VELOCITY + group)

        @pl.when(place * (own - 1 - place) > 0)
        def _():
            arrived(velocity_z.at[comps, pl.ds(1, planes)], VELOCITY + group)

    def beside_arrived(group):
        comps = groups[group]
        arrived(edge.at[comps, :, :, 0], EDGE_LOW + group)
        arrived(edge.at[comps, :, :, 1], EDGE_HIGH + group)

        @pl.when(place > 0)
        def _():
            arrived(velocity_z.at[comps, 0], SIDE_LOW + group)

        @pl.when(place < own - 1)
        def _():
            arrived(velocity_z.at[comps, planes + 1], SIDE_HIGH + group)

    def moved_arrived():
        for _ in range(columns - 1):
            arrived(moved.at[:, pl.ds(0, slab)], MOVED)
            for r in range(2):
                arrived(moved_edge.at[:, pl.ds(0, slab), r], MOVED_EDGE + r)
        arrived(moved_low, LOW)
        arrived(moved_high, HIGH_SIDE)

    def in_lines(values, low, high):
        after = jnp.concatenate([values[:, 1:], high], axis=1)
        before = jnp.concatenate([low, values[:, :-1]], axis=1)
        return before, after

    def slopes():
        lane = lax.broadcasted_iota(jnp.int32, (outer, own, LANES), 2)
        for plane in range(planes):
            here = moved[plane]
            below = moved[plane - 1] if plane > 0 else moved_low[...]
            above = moved[plane + 1] if plane < planes - 1 else moved_high[...]
            slope[0, plane] = 0.5 * (above - below)
            before, after = in_lines(
                here, moved_edge[plane, :, 0:1], moved_edge[plane, :, 1:2]
            )
            slope[1, plane] = 0.5 * (after - before)
            following = jnp.roll(here, -1, 2)
            following = jnp.where(lane == LANES - 1, jnp.roll(following, -1, 0), following)
            previous = jnp.roll(here, 1, 2)
            previous = jnp.where(lane == 0, jnp.roll(previous, 1, 0), previous)
            slope[2, plane] = 0.5 * (following - previous)

    def to_spectrum(group):
        ahead_parts = (ahead[0], ahead[1])
        comps = groups[group]
        for comp in range(comps.start, comps.start + comps.size):
            for plane in range(planes):
                block = velocity_z[comp, plane + 1].reshape(outer * own, LANES)
                spectrum[:, comp, plane] = dot_split(ahead_parts, split_halves(block)).reshape(
                    outer, own, LANES
                )

    def respond():
        for pair in range(outer // 2):
            shape = (components * planes * own, LANES)
            joined = jnp.concatenate(
                [spectrum[2 * pair].reshape(shape), spectrum[2 * pair + 1].reshape(shape)], axis=1
            )
            result = dot_split(split_halves(joined), (pairs[0, pair], pairs[1, pair]))
            shape = (components, planes, own, LANES)
            spectrum[2 * pair] = result[:, :LANES].reshape(shape)
            spectrum[2 * pair + 1] = result[:, LANES:].reshape(shape)

    def from_spectrum(group):
        back_parts = (back[0], back[1])
        comps = groups[group]
        for comp in range(comps.start, comps.start + comps.size):
            for plane in range(planes):
                before, after = in_lines(
                    velocity_z[comp, plane + 1],
                    edge[comp, plane, :, 0:1],
                    edge[comp, plane, :, 1:2],
                )
                sides = (velocity_z[comp, plane] + velocity_z[comp, plane + 2]) + (before + after)
                block = spectrum[:, comp, plane].reshape(outer * own, LANES)
                result = dot_split(back_parts, split_halves(block))
                rest[comp, plane] = result.reshape(outer, own, LANES) - BETA * sides

    send_template()
    send_velocity(0)
    arrived(template_y, TEMPLATE)
    transport_lines()
    send_moved()
    send_velocity(1)
    for load in loads:
        load.wait()
    velocity_arrived(0)
    send_beside(0, True)
    send_target()
    to_spectrum(0)
    velocity_arrived(1)
    send_beside(1, True)
    to_spectrum(1)
    respond()
    moved_arrived()
    slopes()
    for group in range(len(groups)):
        beside_arrived(group)
        from_spectrum(group)
    arrived(target_z, TARGET)
    for plane in range(planes):
        misfit = target_z[plane] - moved[plane]
        for comp in range(components):
            total = rest[comp, plane] + misfit * slope[comp, plane]
            for tile in range(outer):
                out[comp, plane, :, tile * LANES : (tile + 1) * LANES] = total[tile]

    for near, source, sink, kind, to in pending:
        if near is None:
            remote(source, sink, kind, to).wait_send()
        else:

            @pl.when(jnp.logical_not(near))
            def _():
                remote(source, sink, kind, to).wait_send()

    for group in range(len(groups)):
        send_beside(group, False)


def direct(template, target, velocity, departure, weights):
    rows, columns = lax.axis_size("row"), lax.axis_size("col")
    extent_x, _, cells = template.shape
    components = velocity.shape[0]
    planes = extent_x // rows
    lines = rows
    own = lines // columns
    slab = cells // LANES
    outer = slab * columns
    ahead, pairs, back = operators(cells * columns, own)
    tile = (slab, LANES)
    whole = (outer, own, LANES)
    hbm = pl.BlockSpec(memory_space=pl.ANY)
    vmem = pl.BlockSpec(memory_space=pltpu.VMEM)
    smem = pl.BlockSpec(memory_space=pltpu.SMEM)
    kinds = 7 + 5 * 2
    return pl.pallas_call(
        functools.partial(kernel, (rows, columns)),
        out_shape=pltpu.VMEM((components, planes, own, outer * LANES), jnp.float32),
        in_specs=[hbm, hbm, hbm, vmem, smem, hbm, hbm, hbm],
        out_specs=vmem,
        scratch_shapes=[
            pltpu.VMEM((planes, lines) + tile, jnp.float32),
            pltpu.VMEM((planes,) + whole, jnp.float32),
            pltpu.VMEM((components, planes + 2) + whole, jnp.float32),
            pltpu.VMEM((components, planes, outer, SUBLANES, LANES), jnp.float32),
            pltpu.VMEM((planes, columns, slab, own, LANES), jnp.float32),
            pltpu.VMEM((planes, columns, slab, SUBLANES, LANES), jnp.float32),
            pltpu.VMEM((planes,) + whole, jnp.float32),
            pltpu.VMEM((planes, outer, SUBLANES, LANES), jnp.float32),
            pltpu.VMEM(whole, jnp.float32),
            pltpu.VMEM(whole, jnp.float32),
            pltpu.VMEM((components, planes) + whole, jnp.float32),
            pltpu.VMEM((components, planes) + whole, jnp.float32),
            pltpu.VMEM((outer, components, planes, own, LANES), jnp.float32),
            pltpu.VMEM(ahead.shape, jnp.bfloat16),
            pltpu.VMEM(pairs.shape, jnp.bfloat16),
            pltpu.VMEM(back.shape, jnp.bfloat16),
            pltpu.SemaphoreType.DMA((3,)),
            pltpu.SemaphoreType.DMA((kinds,)),
            pltpu.SemaphoreType.DMA((kinds,)),
        ],
        compiler_params=pltpu.CompilerParams(collective_id=0, has_side_effects=True),
    )(
        template.reshape((extent_x,) + tile),
        target.reshape((extent_x,) + tile),
        velocity.reshape((components, extent_x) + tile),
        departure.reshape(departure.shape[:2] + tile),
        weights.T,
        jnp.asarray(ahead),
        jnp.asarray(pairs),
        jnp.asarray(back),
    )


def per_block(template, target, velocity, departure, weights):
    rows, columns = lax.axis_size("row"), lax.axis_size("col")
    components = velocity.shape[0]
    one_line = template.shape[1] == 1 and rows % columns == 0 and columns > 1 and components > 1
    whole_tiles = template.shape[2] % (LANES * SUBLANES) == 0
    short = rows // columns == SUBLANES and template.shape[0] % rows == 0
    if one_line and whole_tiles and short:
        return direct(template, target, velocity, departure, weights)
    return per_device(template, target, velocity, departure, weights)


def solution(mesh):
    in_specs = (
        P(None, "row", "col"),
        P(None, "row", "col"),
        P(None, None, "row", "col"),
        P("row", None, "col"),
        P(),
    )
    out_specs = P(None, "row", "col", None)
    return jax.shard_map(
        per_block, mesh=mesh, in_specs=in_specs, out_specs=out_specs, check_vma=False
    )
```

```python
import functools
import math

import jax
import jax.numpy as jnp
import numpy as np
from jax import lax
from jax.experimental import pallas as pl
from jax.experimental.pallas import tpu as pltpu
from jax.sharding import PartitionSpec as P

QUANT = 8
TAPS = 4


BETA = 0.5
HIGH = lax.Precision.HIGHEST
LANES = 128
SUBLANES = 8
MESH = pl.DeviceIdType.MESH


def with_halo(block, sides, width):
    for axis, dim in sides:
        count = lax.axis_size(axis)
        forward = [(i, i + 1) for i in range(count - 1)]
        forward.append((count - 1, 0))
        backward = [(target, source) for source, target in forward]
        low = lax.ppermute(
            lax.slice_in_dim(block, block.shape[dim] - width, None, axis=dim), axis, forward
        )
        high = lax.ppermute(lax.slice_in_dim(block, 0, width, axis=dim), axis, backward)
        block = jnp.concatenate([low, block, high], axis=dim)
    return block


def central(values, axis):
    return (jnp.roll(values, -1, axis) - jnp.roll(values, 1, axis)) * 0.5


def second_difference(values, axis):
    return 2.0 * values - jnp.roll(values, -1, axis) - jnp.roll(values, 1, axis)


def tap_weights(levels, weight):
    taps = []
    for tap in range(TAPS):
        value = jnp.zeros(levels.shape, jnp.float32)
        for level in range(QUANT):
            value = jnp.where(levels == level, weight(level, tap), value)
        taps.append(value)
    return taps


def transport(template_y, departure, weights):
    planes, lines, columns = template_y.shape
    blocks = departure.shape[1]
    span = lines // blocks
    shift_cells = jnp.floor_divide(departure, QUANT)
    levels = departure - shift_cells * QUANT
    taps = tap_weights(levels, lambda level, tap: weights[level, tap])
    shift = jnp.mod(shift_cells + 1, lines)
    parts = []
    for block in range(blocks):
        rolled = template_y
        step = 1
        while step < lines:
            chosen = (shift[:, block : block + 1] & step) != 0
            rolled = jnp.where(chosen, jnp.roll(rolled, step, 1), rolled)
            step *= 2
        part = 0.0
        for tap in range(TAPS):
            turned = jnp.roll(rolled, -tap - block * span, 1)[:, :span]
            part = part + taps[tap][:, block : block + 1] * turned
        parts.append(part)
    return jnp.concatenate(parts, axis=1)


def curvature(velocity_z):
    field_shape = velocity_z.shape
    length = field_shape[-1]
    inner = 128
    outer = length // inner
    lines = velocity_z.reshape(-1, outer, inner)
    angle = 2.0 * math.pi / length
    outer_index = jnp.arange(outer, dtype=jnp.int32)
    inner_index = jnp.arange(inner, dtype=jnp.int32)
    outer_phase = (
        jnp.mod(outer_index[:, None] * outer_index[None, :] * inner, length).astype(jnp.float32)
        * angle
    )
    cos_outer = jnp.cos(outer_phase)
    sin_outer = jnp.sin(outer_phase)
    twist_phase = (
        jnp.mod(outer_index[:, None] * inner_index[None, :], length).astype(jnp.float32) * angle
    )
    cos_twist = jnp.cos(twist_phase)
    sin_twist = jnp.sin(twist_phase)
    inner_phase = (
        jnp.mod(inner_index[:, None] * inner_index[None, :] * outer, length).astype(jnp.float32)
        * angle
    )
    cos_inner = jnp.cos(inner_phase)
    sin_inner = jnp.sin(inner_phase)
    freq_index = outer_index[:, None] + outer * inner_index[None, :]
    signed = jnp.where(freq_index < length // 2, freq_index, freq_index - length).astype(
        jnp.float32
    )
    symbol = (signed * angle) ** 2 / length
    real_one = jnp.einsum("lap,ak->lkp", lines, cos_outer, precision=HIGH)
    imag_one = -jnp.einsum("lap,ak->lkp", lines, sin_outer, precision=HIGH)
    real_two = real_one * cos_twist + imag_one * sin_twist
    imag_two = imag_one * cos_twist - real_one * sin_twist
    real_three = jnp.einsum("lkp,pq->lkq", real_two, cos_inner, precision=HIGH) + jnp.einsum(
        "lkp,pq->lkq", imag_two, sin_inner, precision=HIGH
    )
    imag_three = jnp.einsum("lkp,pq->lkq", imag_two, cos_inner, precision=HIGH) - jnp.einsum(
        "lkp,pq->lkq", real_two, sin_inner, precision=HIGH
    )
    real_three = real_three * symbol
    imag_three = imag_three * symbol
    real_four = jnp.einsum("lkq,pq->lkp", real_three, cos_inner, precision=HIGH) - jnp.einsum(
        "lkq,pq->lkp", imag_three, sin_inner, precision=HIGH
    )
    imag_four = jnp.einsum("lkq,pq->lkp", imag_three, cos_inner, precision=HIGH) + jnp.einsum(
        "lkq,pq->lkp", real_three, sin_inner, precision=HIGH
    )
    real_five = real_four * cos_twist - imag_four * sin_twist
    imag_five = imag_four * cos_twist + real_four * sin_twist
    result = jnp.einsum("lkp,kn->lnp", real_five, cos_outer, precision=HIGH) - jnp.einsum(
        "lkp,kn->lnp", imag_five, sin_outer, precision=HIGH
    )
    return result.reshape(field_shape)


def spectral(arrived):
    return (arrived, curvature(arrived[3:6]))


def per_device(template, target, velocity, departure, weights):
    across = second_difference(velocity, 1)
    bundle = jnp.concatenate([template[None], target[None], velocity, across], axis=0)
    regrouped = lax.all_to_all(bundle, "row", split_axis=1, concat_axis=2, tiled=True)
    moved_image = transport(regrouped[0], departure, weights)
    misfit = regrouped[1] - moved_image
    pull_along = misfit * central(moved_image, 1)
    velocity_y = regrouped[2:5]
    second_part = second_difference(velocity_y, 2)
    second_part = regrouped[5:8] + second_part
    outgoing = jnp.concatenate(
        [misfit[None], moved_image[None], pull_along[None], velocity_y, second_part], axis=0
    )
    columns_z, bending = spectral(
        lax.all_to_all(outgoing, "col", split_axis=2, concat_axis=3, tiled=True)
    )
    misfit_z = columns_z[0]
    moved_z = columns_z[1]
    second_z = columns_z[6:9]
    padded = with_halo(moved_z, (("row", 0),), 1)
    slope_across = (padded[2:] - padded[:-2]) * 0.5
    force = jnp.stack([misfit_z * slope_across, columns_z[2], misfit_z * central(moved_z, 2)])
    return BETA * (second_z + bending) + force


def split_halves(values):
    high = values.astype(jnp.bfloat16)
    return high, (values - high.astype(jnp.float32)).astype(jnp.bfloat16)


def dot_split(left, right):
    dot = functools.partial(jnp.dot, preferred_element_type=jnp.float32)
    return dot(left[0], right[0]) + (dot(left[0], right[1]) + dot(left[1], right[0]))


def halves_of(matrix):
    high = matrix.astype(np.float32).astype(jnp.bfloat16)
    low = (matrix - high.astype(np.float64)).astype(np.float32).astype(jnp.bfloat16)
    return np.stack([high, low])


def operators(length, rows):
    outer = length // LANES
    frequency = np.fft.fftfreq(length) * length
    response = np.real(np.fft.ifft((2.0 * math.pi / length * frequency) ** 2))
    response[0] += 4.0
    response *= BETA
    inner = np.arange(LANES)
    group = np.arange(outer)
    away = np.mod(
        LANES * group[:, None, None] + inner[None, :, None] - inner[None, None, :], length
    )
    mixed = np.fft.fft(response[away], axis=0)
    pairs = []
    forward = np.zeros((outer, outer))
    inverse = np.zeros((outer, outer))
    forward[0] = 1.0
    forward[1] = (-1.0) ** group
    inverse[:, 0] = 1.0 / outer
    inverse[:, 1] = (-1.0) ** group / outer
    zero = np.zeros((LANES, LANES))
    pairs.append(np.block([[mixed[0].real.T, zero], [zero, mixed[outer // 2].real.T]]))
    for k in range(1, outer // 2):
        real, imag = mixed[k].real.T, mixed[k].imag.T
        pairs.append(np.block([[real, imag], [-imag, real]]))
        phase = 2.0 * math.pi * k * group / outer
        forward[2 * k] = np.cos(phase)
        forward[2 * k + 1] = -np.sin(phase)
        inverse[:, 2 * k] = 2.0 * np.cos(phase) / outer
        inverse[:, 2 * k + 1] = -2.0 * np.sin(phase) / outer
    same = np.eye(rows)
    ahead = np.kron(forward, same)
    back = np.kron(inverse, same)
    return halves_of(ahead), halves_of(np.stack(pairs)), halves_of(back)


def kernel(
    extent,
    template,
    target,
    velocity,
    departure_hbm,
    weights_hbm,
    ahead_hbm,
    pairs_hbm,
    back_hbm,
    out,
    departure,
    weights,
    template_y,
    target_z,
    velocity_z,
    edge,
    extended,
    extended_edge,
    moved,
    moved_edge,
    moved_low,
    moved_high,
    slope,
    rest,
    spectrum,
    ahead,
    pairs,
    back,
    load_sem,
    send_sem,
    recv_sem,
):
    rows, columns = extent
    row, column = lax.axis_index("row"), lax.axis_index("col")
    planes, lines, slab = template_y.shape[:3]
    components = velocity_z.shape[0]
    own = lines // columns
    outer = columns * slab
    owner = row // own
    place = lax.rem(row, own)
    groups = [pl.ds(0, components - 1), pl.ds(components - 1, 1)]
    TEMPLATE, TARGET, MOVED, MOVED_EDGE, LOW, HIGH_SIDE, VELOCITY = 0, 1, 2, 3, 5, 6, 7
    SIDE_LOW, SIDE_HIGH, EDGE_LOW, EDGE_HIGH = (
        VELOCITY + i * len(groups) for i in range(1, 5)
    )
    extent_x = velocity.shape[1]
    here_z = pl.ds(pl.multiple_of(column * slab, slab), slab)

    loads = [
        pltpu.make_async_copy(source, sink, load_sem.at[i])
        for i, (source, sink) in enumerate(
            [
                (departure_hbm, departure),
                (weights_hbm, weights),
                (ahead_hbm, ahead),
                (pairs_hbm, pairs),
                (back_hbm, back),
            ]
        )
    ]

    barrier = pltpu.get_barrier_semaphore()
    for i in range(rows):
        for j in range(columns):
            if i + j > 0:
                pl.semaphore_signal(
                    barrier,
                    inc=1,
                    device_id=(lax.rem(row + i, rows), lax.rem(column + j, columns)),
                    device_id_type=MESH,
                )
    for load in loads:
        load.start()
    pl.semaphore_wait(barrier, rows * columns - 1)

    def remote(source, sink, kind, to):
        return pltpu.make_async_remote_copy(
            src_ref=source,
            dst_ref=sink,
            send_sem=send_sem.at[kind],
            recv_sem=recv_sem.at[kind],
            device_id=to,
            device_id_type=MESH,
        )

    pending = []

    def deliver(source, sink, kind, to, near=None):
        if near is None:
            remote(source, sink, kind, to).start()
        else:

            @pl.when(near)
            def _():
                pltpu.make_async_copy(source, sink, recv_sem.at[kind]).start()

            @pl.when(jnp.logical_not(near))
            def _():
                remote(source, sink, kind, to).start()

        pending.append((near, source, sink, kind, to))

    def arrived(ref, kind):
        pltpu.make_async_copy(ref, ref, recv_sem.at[kind]).wait()

    inside = owner == column
    near = own // 2
    others = []
    for d in [*range(1, columns), 0]:
        for i in range(own):
            spot = i // near * near + lax.rem(place + i, near)
            others.append((d == 0, lax.rem(owner + d, columns) * own + spot))

    def send_template():
        for mine, to in others:
            source = template.at[pl.ds(to * planes, planes)]
            sink = template_y.at[:, row]
            deliver(source, sink, TEMPLATE, (to, column), row == to if mine else None)

    def send_target():
        for mine, to in others:
            deliver(
                target.at[pl.ds(to * planes, planes)],
                target_z.at[:, here_z, place],
                TARGET,
                (to, owner),
                jnp.logical_and(inside, row == to) if mine else None,
            )

    def send_velocity(group):
        comps = groups[group]
        for h in range(columns):
            for to, plane, at in (
                (h * own, (h * own * planes - 1) % extent_x, 0),
                (h * own + own - 1, (h + 1) * own * planes % extent_x, planes + 1),
            ):
                deliver(
                    velocity.at[comps, plane],
                    velocity_z.at[comps, at, here_z, place],
                    VELOCITY + group,
                    (to, owner),
                    jnp.logical_and(inside, row == to),
                )
        for mine, to in others:
            deliver(
                velocity.at[comps, pl.ds(to * planes, planes)],
                velocity_z.at[comps, pl.ds(1, planes), here_z, place],
                VELOCITY + group,
                (to, owner),
                jnp.logical_and(inside, row == to) if mine else None,
            )

    def send_beside(group, start):
        comps = groups[group]
        mine = pl.ds(1, planes)

        def go(*copy):
            if start:
                remote(*copy).start()
            else:
                remote(*copy).wait_send()

        go(
            velocity_z.at[comps, mine, :, own - 1],
            edge.at[comps, :, :, 0],
            EDGE_LOW + group,
            (row, lax.rem(column + 1, columns)),
        )
        go(
            velocity_z.at[comps, mine, :, 0],
            edge.at[comps, :, :, 1],
            EDGE_HIGH + group,
            (row, lax.rem(column + columns - 1, columns)),
        )

        @pl.when(place < own - 1)
        def _():
            go(
                velocity_z.at[comps, planes],
                velocity_z.at[comps, 0],
                SIDE_LOW + group,
                (lax.rem(row + 1, rows), column),
            )

        @pl.when(place > 0)
        def _():
            go(
                velocity_z.at[comps, 1],
                velocity_z.at[comps, planes + 1],
                SIDE_HIGH + group,
                (lax.rem(row + rows - 1, rows), column),
            )

    def transport_lines():
        blocks = departure.shape[1]
        span = lines // blocks
        for plane in range(planes):
            image = [template_y[plane, y] for y in range(lines)]
            values = []
            for block in range(blocks):
                offset = departure[plane, block]
                whole = offset >> (QUANT.bit_length() - 1)
                levels = offset - whole * QUANT
                taps = tap_weights(levels, lambda level, tap: weights[tap, level])
                shift = jnp.where(whole + 1 < 0, whole + 1 + lines, whole + 1)
                rolled = image
                step = 1
                while step < lines:
                    chosen = (shift & step) != 0
                    rolled = [
                        jnp.where(chosen, rolled[(y - step) % lines], rolled[y])
                        for y in range(lines)
                    ]
                    step *= 2
                for y in range(block * span, (block + 1) * span):
                    value = taps[0] * rolled[y]
                    for tap in range(1, TAPS):
                        value = value + taps[tap] * rolled[(y + tap) % lines]
                    values.append(value)
            for y in range(lines):
                extended[plane, y // own, :, y % own, :] = values[y]
            for j in range(columns):
                extended_edge[plane, j, :, 0, :] = values[(j * own - 1) % lines]
                extended_edge[plane, j, :, 1, :] = values[(j * own + own) % lines]

    def send_moved():
        up, down = lax.rem(row + 1, rows), lax.rem(row + rows - 1, rows)
        for j in range(columns):
            to = lax.rem(column + j, columns)
            deliver(extended.at[planes - 1, to], moved_low.at[here_z], LOW, (up, to))
            deliver(extended.at[0, to], moved_high.at[here_z], HIGH_SIDE, (down, to))
            if j > 0:
                deliver(extended.at[:, to], moved.at[:, here_z], MOVED, (row, to))
                for r in range(2):
                    deliver(
                        extended_edge.at[:, to, :, r],
                        moved_edge.at[:, here_z, r],
                        MOVED_EDGE + r,
                        (row, to),
                    )
        moved[:, here_z] = extended[:, column]
        moved_edge[:, here_z] = extended_edge[:, column]

    def velocity_arrived(group):
        comps = groups[group]

        @pl.when(place == 0)
        def _():
            arrived(velocity_z.at[comps, pl.ds(0, planes + 1)], VELOCITY + group)

        @pl.when(place == own - 1)
        def _():
            arrived(velocity_z.at[comps, pl.ds(1, planes + 1)], VELOCITY + group)

        @pl.when(place * (own - 1 - place) > 0)
        def _():
            arrived(velocity_z.at[comps, pl.ds(1, planes)], VELOCITY + group)

    def beside_arrived(group):
        comps = groups[group]
        arrived(edge.at[comps, :, :, 0], EDGE_LOW + group)
        arrived(edge.at[comps, :, :, 1], EDGE_HIGH + group)

        @pl.when(place > 0)
        def _():
            arrived(velocity_z.at[comps, 0], SIDE_LOW + group)

        @pl.when(place < own - 1)
        def _():
            arrived(velocity_z.at[comps, planes + 1], SIDE_HIGH + group)

    def moved_arrived():
        for _ in range(columns - 1):
            arrived(moved.at[:, pl.ds(0, slab)], MOVED)
            for r in range(2):
                arrived(moved_edge.at[:, pl.ds(0, slab), r], MOVED_EDGE + r)
        arrived(moved_low, LOW)
        arrived(moved_high, HIGH_SIDE)

    def in_lines(values, low, high):
        after = jnp.concatenate([values[:, 1:], high], axis=1)
        before = jnp.concatenate([low, values[:, :-1]], axis=1)
        return before, after

    def slopes():
        lane = lax.broadcasted_iota(jnp.int32, (outer, own, LANES), 2)
        for plane in range(planes):
            here = moved[plane]
            below = moved[plane - 1] if plane > 0 else moved_low[...]
            above = moved[plane + 1] if plane < planes - 1 else moved_high[...]
            slope[0, plane] = 0.5 * (above - below)
            before, after = in_lines(
                here, moved_edge[plane, :, 0:1], moved_edge[plane, :, 1:2]
            )
            slope[1, plane] = 0.5 * (after - before)
            following = jnp.roll(here, -1, 2)
            following = jnp.where(lane == LANES - 1, jnp.roll(following, -1, 0), following)
            previous = jnp.roll(here, 1, 2)
            previous = jnp.where(lane == 0, jnp.roll(previous, 1, 0), previous)
            slope[2, plane] = 0.5 * (following - previous)

    def to_spectrum(group):
        ahead_parts = (ahead[0], ahead[1])
        comps = groups[group]
        for comp in range(comps.start, comps.start + comps.size):
            for plane in range(planes):
                block = velocity_z[comp, plane + 1].reshape(outer * own, LANES)
                spectrum[:, comp, plane] = dot_split(ahead_parts, split_halves(block)).reshape(
                    outer, own, LANES
                )

    def respond():
        for pair in range(outer // 2):
            shape = (components * planes * own, LANES)
            joined = jnp.concatenate(
                [spectrum[2 * pair].reshape(shape), spectrum[2 * pair + 1].reshape(shape)], axis=1
            )
            result = dot_split(split_halves(joined), (pairs[0, pair], pairs[1, pair]))
            shape = (components, planes, own, LANES)
            spectrum[2 * pair] = result[:, :LANES].reshape(shape)
            spectrum[2 * pair + 1] = result[:, LANES:].reshape(shape)

    def from_spectrum(group):
        back_parts = (back[0], back[1])
        comps = groups[group]
        for comp in range(comps.start, comps.start + comps.size):
            for plane in range(planes):
                before, after = in_lines(
                    velocity_z[comp, plane + 1],
                    edge[comp, plane, :, 0:1],
                    edge[comp, plane, :, 1:2],
                )
                sides = (velocity_z[comp, plane] + velocity_z[comp, plane + 2]) + (before + after)
                block = spectrum[:, comp, plane].reshape(outer * own, LANES)
                result = dot_split(back_parts, split_halves(block))
                rest[comp, plane] = result.reshape(outer, own, LANES) - BETA * sides

    send_template()
    send_velocity(0)
    for load in loads:
        load.wait()
    arrived(template_y, TEMPLATE)
    transport_lines()
    send_moved()
    send_velocity(1)
    velocity_arrived(0)
    send_beside(0, True)
    send_target()
    to_spectrum(0)
    velocity_arrived(1)
    send_beside(1, True)
    to_spectrum(1)
    respond()
    moved_arrived()
    slopes()
    for group in range(len(groups)):
        beside_arrived(group)
        from_spectrum(group)
    arrived(target_z, TARGET)
    for plane in range(planes):
        misfit = target_z[plane] - moved[plane]
        for comp in range(components):
            total = rest[comp, plane] + misfit * slope[comp, plane]
            for tile in range(outer):
                out[comp, plane, :, tile * LANES : (tile + 1) * LANES] = total[tile]

    for near, source, sink, kind, to in pending:
        if near is None:
            remote(source, sink, kind, to).wait_send()
        else:

            @pl.when(jnp.logical_not(near))
            def _():
                remote(source, sink, kind, to).wait_send()

    for group in range(len(groups)):
        send_beside(group, False)


def direct(template, target, velocity, departure, weights):
    rows, columns = lax.axis_size("row"), lax.axis_size("col")
    extent_x, _, cells = template.shape
    components = velocity.shape[0]
    planes = extent_x // rows
    lines = rows
    own = lines // columns
    slab = cells // LANES
    outer = slab * columns
    ahead, pairs, back = operators(cells * columns, own)
    tile = (slab, LANES)
    whole = (outer, own, LANES)
    hbm = pl.BlockSpec(memory_space=pl.ANY)
    vmem = pl.BlockSpec(memory_space=pltpu.VMEM)
    kinds = 7 + 5 * 2
    return pl.pallas_call(
        functools.partial(kernel, (rows, columns)),
        out_shape=pltpu.VMEM((components, planes, own, outer * LANES), jnp.float32),
        in_specs=[hbm] * 8,
        out_specs=vmem,
        scratch_shapes=[
            pltpu.VMEM(departure.shape[:2] + tile, jnp.int32),
            pltpu.SMEM(weights.shape[::-1], jnp.float32),
            pltpu.VMEM((planes, lines) + tile, jnp.float32),
            pltpu.VMEM((planes,) + whole, jnp.float32),
            pltpu.VMEM((components, planes + 2) + whole, jnp.float32),
            pltpu.VMEM((components, planes, outer, SUBLANES, LANES), jnp.float32),
            pltpu.VMEM((planes, columns, slab, own, LANES), jnp.float32),
            pltpu.VMEM((planes, columns, slab, SUBLANES, LANES), jnp.float32),
            pltpu.VMEM((planes,) + whole, jnp.float32),
            pltpu.VMEM((planes, outer, SUBLANES, LANES), jnp.float32),
            pltpu.VMEM(whole, jnp.float32),
            pltpu.VMEM(whole, jnp.float32),
            pltpu.VMEM((components, planes) + whole, jnp.float32),
            pltpu.VMEM((components, planes) + whole, jnp.float32),
            pltpu.VMEM((outer, components, planes, own, LANES), jnp.float32),
            pltpu.VMEM(ahead.shape, jnp.bfloat16),
            pltpu.VMEM(pairs.shape, jnp.bfloat16),
            pltpu.VMEM(back.shape, jnp.bfloat16),
            pltpu.SemaphoreType.DMA((5,)),
            pltpu.SemaphoreType.DMA((kinds,)),
            pltpu.SemaphoreType.DMA((kinds,)),
        ],
        compiler_params=pltpu.CompilerParams(collective_id=0, has_side_effects=True),
    )(
        template.reshape((extent_x,) + tile),
        target.reshape((extent_x,) + tile),
        velocity.reshape((components, extent_x) + tile),
        departure.reshape(departure.shape[:2] + tile),
        weights.T,
        jnp.asarray(ahead),
        jnp.asarray(pairs),
        jnp.asarray(back),
    )


def per_block(template, target, velocity, departure, weights):
    rows, columns = lax.axis_size("row"), lax.axis_size("col")
    components = velocity.shape[0]
    one_line = template.shape[1] == 1 and rows % columns == 0 and columns > 1 and components > 1
    whole_tiles = template.shape[2] % (LANES * SUBLANES) == 0
    short = rows // columns == SUBLANES and template.shape[0] % rows == 0
    if one_line and whole_tiles and short:
        return direct(template, target, velocity, departure, weights)
    return per_device(template, target, velocity, departure, weights)


def solution(mesh):
    in_specs = (
        P(None, "row", "col"),
        P(None, "row", "col"),
        P(None, None, "row", "col"),
        P("row", None, "col"),
        P(),
    )
    out_specs = P(None, "row", "col", None)
    return jax.shard_map(
        per_block, mesh=mesh, in_specs=in_specs, out_specs=out_specs, check_vma=False
    )
```

```python
import functools
import math

import jax
import jax.numpy as jnp
import numpy as np
from jax import lax
from jax.experimental import pallas as pl
from jax.experimental.pallas import tpu as pltpu
from jax.sharding import PartitionSpec as P

QUANT = 8
TAPS = 4


BETA = 0.5
HIGH = lax.Precision.HIGHEST
LANES = 128
SUBLANES = 8
MESH = pl.DeviceIdType.MESH


def with_halo(block, sides, width):
    for axis, dim in sides:
        count = lax.axis_size(axis)
        forward = [(i, i + 1) for i in range(count - 1)]
        forward.append((count - 1, 0))
        backward = [(target, source) for source, target in forward]
        low = lax.ppermute(
            lax.slice_in_dim(block, block.shape[dim] - width, None, axis=dim), axis, forward
        )
        high = lax.ppermute(lax.slice_in_dim(block, 0, width, axis=dim), axis, backward)
        block = jnp.concatenate([low, block, high], axis=dim)
    return block


def central(values, axis):
    return (jnp.roll(values, -1, axis) - jnp.roll(values, 1, axis)) * 0.5


def second_difference(values, axis):
    return 2.0 * values - jnp.roll(values, -1, axis) - jnp.roll(values, 1, axis)


def tap_weights(levels, weight):
    taps = []
    for tap in range(TAPS):
        value = jnp.zeros(levels.shape, jnp.float32)
        for level in range(QUANT):
            value = jnp.where(levels == level, weight(level, tap), value)
        taps.append(value)
    return taps


def transport(template_y, departure, weights):
    planes, lines, columns = template_y.shape
    blocks = departure.shape[1]
    span = lines // blocks
    shift_cells = jnp.floor_divide(departure, QUANT)
    levels = departure - shift_cells * QUANT
    taps = tap_weights(levels, lambda level, tap: weights[level, tap])
    shift = jnp.mod(shift_cells + 1, lines)
    parts = []
    for block in range(blocks):
        rolled = template_y
        step = 1
        while step < lines:
            chosen = (shift[:, block : block + 1] & step) != 0
            rolled = jnp.where(chosen, jnp.roll(rolled, step, 1), rolled)
            step *= 2
        part = 0.0
        for tap in range(TAPS):
            turned = jnp.roll(rolled, -tap - block * span, 1)[:, :span]
            part = part + taps[tap][:, block : block + 1] * turned
        parts.append(part)
    return jnp.concatenate(parts, axis=1)


def curvature(velocity_z):
    field_shape = velocity_z.shape
    length = field_shape[-1]
    inner = 128
    outer = length // inner
    lines = velocity_z.reshape(-1, outer, inner)
    angle = 2.0 * math.pi / length
    outer_index = jnp.arange(outer, dtype=jnp.int32)
    inner_index = jnp.arange(inner, dtype=jnp.int32)
    outer_phase = (
        jnp.mod(outer_index[:, None] * outer_index[None, :] * inner, length).astype(jnp.float32)
        * angle
    )
    cos_outer = jnp.cos(outer_phase)
    sin_outer = jnp.sin(outer_phase)
    twist_phase = (
        jnp.mod(outer_index[:, None] * inner_index[None, :], length).astype(jnp.float32) * angle
    )
    cos_twist = jnp.cos(twist_phase)
    sin_twist = jnp.sin(twist_phase)
    inner_phase = (
        jnp.mod(inner_index[:, None] * inner_index[None, :] * outer, length).astype(jnp.float32)
        * angle
    )
    cos_inner = jnp.cos(inner_phase)
    sin_inner = jnp.sin(inner_phase)
    freq_index = outer_index[:, None] + outer * inner_index[None, :]
    signed = jnp.where(freq_index < length // 2, freq_index, freq_index - length).astype(
        jnp.float32
    )
    symbol = (signed * angle) ** 2 / length
    real_one = jnp.einsum("lap,ak->lkp", lines, cos_outer, precision=HIGH)
    imag_one = -jnp.einsum("lap,ak->lkp", lines, sin_outer, precision=HIGH)
    real_two = real_one * cos_twist + imag_one * sin_twist
    imag_two = imag_one * cos_twist - real_one * sin_twist
    real_three = jnp.einsum("lkp,pq->lkq", real_two, cos_inner, precision=HIGH) + jnp.einsum(
        "lkp,pq->lkq", imag_two, sin_inner, precision=HIGH
    )
    imag_three = jnp.einsum("lkp,pq->lkq", imag_two, cos_inner, precision=HIGH) - jnp.einsum(
        "lkp,pq->lkq", real_two, sin_inner, precision=HIGH
    )
    real_three = real_three * symbol
    imag_three = imag_three * symbol
    real_four = jnp.einsum("lkq,pq->lkp", real_three, cos_inner, precision=HIGH) - jnp.einsum(
        "lkq,pq->lkp", imag_three, sin_inner, precision=HIGH
    )
    imag_four = jnp.einsum("lkq,pq->lkp", imag_three, cos_inner, precision=HIGH) + jnp.einsum(
        "lkq,pq->lkp", real_three, sin_inner, precision=HIGH
    )
    real_five = real_four * cos_twist - imag_four * sin_twist
    imag_five = imag_four * cos_twist + real_four * sin_twist
    result = jnp.einsum("lkp,kn->lnp", real_five, cos_outer, precision=HIGH) - jnp.einsum(
        "lkp,kn->lnp", imag_five, sin_outer, precision=HIGH
    )
    return result.reshape(field_shape)


def spectral(arrived):
    return (arrived, curvature(arrived[3:6]))


def per_device(template, target, velocity, departure, weights):
    across = second_difference(velocity, 1)
    bundle = jnp.concatenate([template[None], target[None], velocity, across], axis=0)
    regrouped = lax.all_to_all(bundle, "row", split_axis=1, concat_axis=2, tiled=True)
    moved_image = transport(regrouped[0], departure, weights)
    misfit = regrouped[1] - moved_image
    pull_along = misfit * central(moved_image, 1)
    velocity_y = regrouped[2:5]
    second_part = second_difference(velocity_y, 2)
    second_part = regrouped[5:8] + second_part
    outgoing = jnp.concatenate(
        [misfit[None], moved_image[None], pull_along[None], velocity_y, second_part], axis=0
    )
    columns_z, bending = spectral(
        lax.all_to_all(outgoing, "col", split_axis=2, concat_axis=3, tiled=True)
    )
    misfit_z = columns_z[0]
    moved_z = columns_z[1]
    second_z = columns_z[6:9]
    padded = with_halo(moved_z, (("row", 0),), 1)
    slope_across = (padded[2:] - padded[:-2]) * 0.5
    force = jnp.stack([misfit_z * slope_across, columns_z[2], misfit_z * central(moved_z, 2)])
    return BETA * (second_z + bending) + force


def split_halves(values):
    high = values.astype(jnp.bfloat16)
    return high, (values - high.astype(jnp.float32)).astype(jnp.bfloat16)


def dot_split(left, right):
    dot = functools.partial(jnp.dot, preferred_element_type=jnp.float32)
    return dot(left[0], right[0]) + (dot(left[0], right[1]) + dot(left[1], right[0]))


def halves_of(matrix):
    high = matrix.astype(np.float32).astype(jnp.bfloat16)
    low = (matrix - high.astype(np.float64)).astype(np.float32).astype(jnp.bfloat16)
    return np.stack([high, low])


def operators(length, rows):
    outer = length // LANES
    frequency = np.fft.fftfreq(length) * length
    response = np.real(np.fft.ifft((2.0 * math.pi / length * frequency) ** 2))
    response[0] += 4.0
    response *= BETA
    inner = np.arange(LANES)
    group = np.arange(outer)
    away = np.mod(
        LANES * group[:, None, None] + inner[None, :, None] - inner[None, None, :], length
    )
    mixed = np.fft.fft(response[away], axis=0)
    pairs = []
    forward = np.zeros((outer, outer))
    inverse = np.zeros((outer, outer))
    forward[0] = 1.0
    forward[1] = (-1.0) ** group
    inverse[:, 0] = 1.0 / outer
    inverse[:, 1] = (-1.0) ** group / outer
    zero = np.zeros((LANES, LANES))
    pairs.append(np.block([[mixed[0].real.T, zero], [zero, mixed[outer // 2].real.T]]))
    for k in range(1, outer // 2):
        real, imag = mixed[k].real.T, mixed[k].imag.T
        pairs.append(np.block([[real, imag], [-imag, real]]))
        phase = 2.0 * math.pi * k * group / outer
        forward[2 * k] = np.cos(phase)
        forward[2 * k + 1] = -np.sin(phase)
        inverse[:, 2 * k] = 2.0 * np.cos(phase) / outer
        inverse[:, 2 * k + 1] = -2.0 * np.sin(phase) / outer
    same = np.eye(rows)
    ahead = np.kron(forward, same)
    back = np.kron(inverse, same)
    return halves_of(ahead), halves_of(np.stack(pairs)), halves_of(back)


def kernel(
    extent,
    template,
    target,
    velocity,
    departure_hbm,
    weights_hbm,
    ahead_hbm,
    pairs_hbm,
    back_hbm,
    out,
    departure,
    weights,
    template_y,
    target_z,
    velocity_z,
    edge,
    extended,
    extended_edge,
    moved,
    moved_edge,
    moved_low,
    moved_high,
    slope,
    rest,
    spectrum,
    ahead,
    pairs,
    back,
    load_sem,
    send_sem,
    recv_sem,
    ready_sem,
):
    rows, columns = extent
    row, column = lax.axis_index("row"), lax.axis_index("col")
    planes, lines, slab = template_y.shape[:3]
    components = velocity_z.shape[0]
    own = lines // columns
    outer = columns * slab
    owner = row // own
    place = lax.rem(row, own)
    groups = [pl.ds(0, components - 1), pl.ds(components - 1, 1)]
    TEMPLATE, TARGET, MOVED, MOVED_EDGE, LOW, HIGH_SIDE, VELOCITY = 0, 1, 2, 3, 5, 6, 7
    SIDE_LOW, SIDE_HIGH, EDGE_LOW, EDGE_HIGH = (
        VELOCITY + i * len(groups) for i in range(1, 5)
    )
    extent_x = velocity.shape[1]
    here_z = pl.ds(pl.multiple_of(column * slab, slab), slab)

    loads = [
        pltpu.make_async_copy(source, sink, load_sem.at[i])
        for i, (source, sink) in enumerate(
            [
                (departure_hbm, departure),
                (weights_hbm, weights),
                (ahead_hbm, ahead),
                (pairs_hbm, pairs),
                (back_hbm, back),
            ]
        )
    ]

    near = own // 2
    here = lax.rem(row, near)
    line = [
        (lax.rem(row + i * near, rows), lax.rem(column + j, columns))
        for i in range(rows // near)
        for j in range(columns)
        if i + j > 0
    ]
    beside = [(row - here + lax.rem(here + i, near), column) for i in range(1, near)]
    barrier = pltpu.get_barrier_semaphore()
    for device in line + beside:
        pl.semaphore_signal(barrier, inc=1, device_id=device, device_id_type=MESH)
    for load in loads:
        load.start()
    pl.semaphore_wait(barrier, len(line) + len(beside))
    for device in beside:
        pl.semaphore_signal(ready_sem, inc=1, device_id=device, device_id_type=MESH)

    def remote(source, sink, kind, to):
        return pltpu.make_async_remote_copy(
            src_ref=source,
            dst_ref=sink,
            send_sem=send_sem.at[kind],
            recv_sem=recv_sem.at[kind],
            device_id=to,
            device_id_type=MESH,
        )

    sending = [True]

    def deliver(source, sink, kind, to, stays=None):
        def go():
            copy = remote(source, sink, kind, to)
            if sending[0]:
                copy.start()
            else:
                copy.wait_send()

        if stays is None:
            go()
            return
        pl.when(jnp.logical_not(stays))(go)
        if sending[0]:

            @pl.when(stays)
            def _():
                pltpu.make_async_copy(source, sink, recv_sem.at[kind]).start()

    def arrived(ref, kind):
        pltpu.make_async_copy(ref, ref, recv_sem.at[kind]).wait()

    inside = owner == column
    early, others = [], []
    for d in [*range(1, columns), 0]:
        for i in range(own):
            spot = i // near * near + lax.rem(place + i, near)
            group = early if d > 0 and i % near == 0 else others
            group.append((d == 0, lax.rem(owner + d, columns) * own + spot))

    def send_template(rows_of):
        for mine, to in rows_of:
            source = template.at[pl.ds(to * planes, planes)]
            sink = template_y.at[:, row]
            deliver(source, sink, TEMPLATE, (to, column), row == to if mine else None)

    def send_target(rows_of):
        for mine, to in rows_of:
            deliver(
                target.at[pl.ds(to * planes, planes)],
                target_z.at[:, here_z, place],
                TARGET,
                (to, owner),
                jnp.logical_and(inside, row == to) if mine else None,
            )

    def send_velocity(group, rows_of):
        comps = groups[group]
        for mine, to in rows_of:
            deliver(
                velocity.at[comps, pl.ds(to * planes, planes)],
                velocity_z.at[comps, pl.ds(1, planes), here_z, place],
                VELOCITY + group,
                (to, owner),
                jnp.logical_and(inside, row == to) if mine else None,
            )

    def send_halo(group):
        comps = groups[group]
        for h in range(columns):
            for to, plane, at in (
                (h * own, (h * own * planes - 1) % extent_x, 0),
                (h * own + own - 1, (h + 1) * own * planes % extent_x, planes + 1),
            ):
                deliver(
                    velocity.at[comps, plane],
                    velocity_z.at[comps, at, here_z, place],
                    VELOCITY + group,
                    (to, owner),
                    jnp.logical_and(inside, row == to),
                )

    def send_beside(group, start):
        comps = groups[group]
        mine = pl.ds(1, planes)

        def go(*copy):
            if start:
                remote(*copy).start()
            else:
                remote(*copy).wait_send()

        go(
            velocity_z.at[comps, mine, :, own - 1],
            edge.at[comps, :, :, 0],
            EDGE_LOW + group,
            (row, lax.rem(column + 1, columns)),
        )
        go(
            velocity_z.at[comps, mine, :, 0],
            edge.at[comps, :, :, 1],
            EDGE_HIGH + group,
            (row, lax.rem(column + columns - 1, columns)),
        )

        @pl.when(place < own - 1)
        def _():
            go(
                velocity_z.at[comps, planes],
                velocity_z.at[comps, 0],
                SIDE_LOW + group,
                (lax.rem(row + 1, rows), column),
            )

        @pl.when(place > 0)
        def _():
            go(
                velocity_z.at[comps, 1],
                velocity_z.at[comps, planes + 1],
                SIDE_HIGH + group,
                (lax.rem(row + rows - 1, rows), column),
            )

    def transport_lines():
        blocks = departure.shape[1]
        span = lines // blocks
        for plane in range(planes):
            image = [template_y[plane, y] for y in range(lines)]
            values = []
            for block in range(blocks):
                offset = departure[plane, block]
                whole = offset >> (QUANT.bit_length() - 1)
                levels = offset - whole * QUANT
                taps = tap_weights(levels, lambda level, tap: weights[tap, level])
                shift = jnp.where(whole + 1 < 0, whole + 1 + lines, whole + 1)
                rolled = image
                step = 1
                while step < lines:
                    chosen = (shift & step) != 0
                    rolled = [
                        jnp.where(chosen, rolled[(y - step) % lines], rolled[y])
                        for y in range(lines)
                    ]
                    step *= 2
                for y in range(block * span, (block + 1) * span):
                    value = taps[0] * rolled[y]
                    for tap in range(1, TAPS):
                        value = value + taps[tap] * rolled[(y + tap) % lines]
                    values.append(value)
            for y in range(lines):
                extended[plane, y // own, :, y % own, :] = values[y]
            for j in range(columns):
                extended_edge[plane, j, :, 0, :] = values[(j * own - 1) % lines]
                extended_edge[plane, j, :, 1, :] = values[(j * own + own) % lines]

    def send_moved():
        up, down = lax.rem(row + 1, rows), lax.rem(row + rows - 1, rows)
        for j in range(columns):
            to = lax.rem(column + j, columns)
            deliver(extended.at[planes - 1, to], moved_low.at[here_z], LOW, (up, to))
            deliver(extended.at[0, to], moved_high.at[here_z], HIGH_SIDE, (down, to))
            if j > 0:
                deliver(extended.at[:, to], moved.at[:, here_z], MOVED, (row, to))
                for r in range(2):
                    deliver(
                        extended_edge.at[:, to, :, r],
                        moved_edge.at[:, here_z, r],
                        MOVED_EDGE + r,
                        (row, to),
                    )
    def velocity_arrived(group):
        comps = groups[group]

        @pl.when(place == 0)
        def _():
            arrived(velocity_z.at[comps, pl.ds(0, planes + 1)], VELOCITY + group)

        @pl.when(place == own - 1)
        def _():
            arrived(velocity_z.at[comps, pl.ds(1, planes + 1)], VELOCITY + group)

        @pl.when(place * (own - 1 - place) > 0)
        def _():
            arrived(velocity_z.at[comps, pl.ds(1, planes)], VELOCITY + group)

    def beside_arrived(group):
        comps = groups[group]
        arrived(edge.at[comps, :, :, 0], EDGE_LOW + group)
        arrived(edge.at[comps, :, :, 1], EDGE_HIGH + group)

        @pl.when(place > 0)
        def _():
            arrived(velocity_z.at[comps, 0], SIDE_LOW + group)

        @pl.when(place < own - 1)
        def _():
            arrived(velocity_z.at[comps, planes + 1], SIDE_HIGH + group)

    def moved_arrived():
        for _ in range(columns - 1):
            arrived(moved.at[:, pl.ds(0, slab)], MOVED)
            for r in range(2):
                arrived(moved_edge.at[:, pl.ds(0, slab), r], MOVED_EDGE + r)
        arrived(moved_low, LOW)
        arrived(moved_high, HIGH_SIDE)

    def in_lines(values, low, high):
        after = jnp.concatenate([values[:, 1:], high], axis=1)
        before = jnp.concatenate([low, values[:, :-1]], axis=1)
        return before, after

    def slopes():
        lane = lax.broadcasted_iota(jnp.int32, (outer, own, LANES), 2)
        for plane in range(planes):
            here = moved[plane]
            below = moved[plane - 1] if plane > 0 else moved_low[...]
            above = moved[plane + 1] if plane < planes - 1 else moved_high[...]
            slope[0, plane] = 0.5 * (above - below)
            before, after = in_lines(
                here, moved_edge[plane, :, 0:1], moved_edge[plane, :, 1:2]
            )
            slope[1, plane] = 0.5 * (after - before)
            following = jnp.roll(here, -1, 2)
            following = jnp.where(lane == LANES - 1, jnp.roll(following, -1, 0), following)
            previous = jnp.roll(here, 1, 2)
            previous = jnp.where(lane == 0, jnp.roll(previous, 1, 0), previous)
            slope[2, plane] = 0.5 * (following - previous)

    def to_spectrum(group):
        ahead_parts = (ahead[0], ahead[1])
        comps = groups[group]
        for comp in range(comps.start, comps.start + comps.size):
            for plane in range(planes):
                block = velocity_z[comp, plane + 1].reshape(outer * own, LANES)
                spectrum[:, comp, plane] = dot_split(ahead_parts, split_halves(block)).reshape(
                    outer, own, LANES
                )

    def respond():
        for pair in range(outer // 2):
            shape = (components * planes * own, LANES)
            joined = jnp.concatenate(
                [spectrum[2 * pair].reshape(shape), spectrum[2 * pair + 1].reshape(shape)], axis=1
            )
            result = dot_split(split_halves(joined), (pairs[0, pair], pairs[1, pair]))
            shape = (components, planes, own, LANES)
            spectrum[2 * pair] = result[:, :LANES].reshape(shape)
            spectrum[2 * pair + 1] = result[:, LANES:].reshape(shape)

    def from_spectrum(group):
        back_parts = (back[0], back[1])
        comps = groups[group]
        for comp in range(comps.start, comps.start + comps.size):
            for plane in range(planes):
                before, after = in_lines(
                    velocity_z[comp, plane + 1],
                    edge[comp, plane, :, 0:1],
                    edge[comp, plane, :, 1:2],
                )
                sides = (velocity_z[comp, plane] + velocity_z[comp, plane + 2]) + (before + after)
                block = spectrum[:, comp, plane].reshape(outer * own, LANES)
                result = dot_split(back_parts, split_halves(block))
                rest[comp, plane] = result.reshape(outer, own, LANES) - BETA * sides

    send_template(early)
    send_velocity(0, early)
    pl.semaphore_wait(ready_sem, len(beside))
    send_template(others)
    send_halo(0)
    send_velocity(0, others)
    send_velocity(1, early)
    send_halo(1)
    send_velocity(1, others)
    for load in loads:
        load.wait()
    arrived(template_y, TEMPLATE)
    transport_lines()
    send_moved()
    moved[:, here_z] = extended[:, column]
    moved_edge[:, here_z] = extended_edge[:, column]
    velocity_arrived(0)
    send_beside(0, True)
    send_target(early)
    send_target(others)
    to_spectrum(0)
    velocity_arrived(1)
    send_beside(1, True)
    to_spectrum(1)
    respond()
    moved_arrived()
    slopes()
    for group in range(len(groups)):
        beside_arrived(group)
        from_spectrum(group)
    arrived(target_z, TARGET)
    for plane in range(planes):
        misfit = target_z[plane] - moved[plane]
        for comp in range(components):
            total = rest[comp, plane] + misfit * slope[comp, plane]
            for tile in range(outer):
                out[comp, plane, :, tile * LANES : (tile + 1) * LANES] = total[tile]

    sending[0] = False
    for rows_of in (early, others):
        send_template(rows_of)
        send_target(rows_of)
        for group in range(len(groups)):
            send_velocity(group, rows_of)
    send_moved()
    for group in range(len(groups)):
        send_halo(group)
        send_beside(group, False)


def direct(template, target, velocity, departure, weights):
    rows, columns = lax.axis_size("row"), lax.axis_size("col")
    extent_x, _, cells = template.shape
    components = velocity.shape[0]
    planes = extent_x // rows
    lines = rows
    own = lines // columns
    slab = cells // LANES
    outer = slab * columns
    ahead, pairs, back = operators(cells * columns, own)
    tile = (slab, LANES)
    whole = (outer, own, LANES)
    hbm = pl.BlockSpec(memory_space=pl.ANY)
    vmem = pl.BlockSpec(memory_space=pltpu.VMEM)
    kinds = 7 + 5 * 2
    return pl.pallas_call(
        functools.partial(kernel, (rows, columns)),
        out_shape=pltpu.VMEM((components, planes, own, outer * LANES), jnp.float32),
        in_specs=[hbm] * 8,
        out_specs=vmem,
        scratch_shapes=[
            pltpu.VMEM(departure.shape[:2] + tile, jnp.int32),
            pltpu.SMEM(weights.shape[::-1], jnp.float32),
            pltpu.VMEM((planes, lines) + tile, jnp.float32),
            pltpu.VMEM((planes,) + whole, jnp.float32),
            pltpu.VMEM((components, planes + 2) + whole, jnp.float32),
            pltpu.VMEM((components, planes, outer, SUBLANES, LANES), jnp.float32),
            pltpu.VMEM((planes, columns, slab, own, LANES), jnp.float32),
            pltpu.VMEM((planes, columns, slab, SUBLANES, LANES), jnp.float32),
            pltpu.VMEM((planes,) + whole, jnp.float32),
            pltpu.VMEM((planes, outer, SUBLANES, LANES), jnp.float32),
            pltpu.VMEM(whole, jnp.float32),
            pltpu.VMEM(whole, jnp.float32),
            pltpu.VMEM((components, planes) + whole, jnp.float32),
            pltpu.VMEM((components, planes) + whole, jnp.float32),
            pltpu.VMEM((outer, components, planes, own, LANES), jnp.float32),
            pltpu.VMEM(ahead.shape, jnp.bfloat16),
            pltpu.VMEM(pairs.shape, jnp.bfloat16),
            pltpu.VMEM(back.shape, jnp.bfloat16),
            pltpu.SemaphoreType.DMA((5,)),
            pltpu.SemaphoreType.DMA((kinds,)),
            pltpu.SemaphoreType.DMA((kinds,)),
            pltpu.SemaphoreType.REGULAR,
        ],
        compiler_params=pltpu.CompilerParams(collective_id=0, has_side_effects=True),
    )(
        template.reshape((extent_x,) + tile),
        target.reshape((extent_x,) + tile),
        velocity.reshape((components, extent_x) + tile),
        departure.reshape(departure.shape[:2] + tile),
        weights.T,
        jnp.asarray(ahead),
        jnp.asarray(pairs),
        jnp.asarray(back),
    )


def per_block(template, target, velocity, departure, weights):
    rows, columns = lax.axis_size("row"), lax.axis_size("col")
    components = velocity.shape[0]
    one_line = template.shape[1] == 1 and rows % columns == 0 and columns > 1 and components > 1
    whole_tiles = template.shape[2] % (LANES * SUBLANES) == 0
    short = rows // columns == SUBLANES and template.shape[0] % rows == 0
    if one_line and whole_tiles and short:
        return direct(template, target, velocity, departure, weights)
    return per_device(template, target, velocity, departure, weights)


def solution(mesh):
    in_specs = (
        P(None, "row", "col"),
        P(None, "row", "col"),
        P(None, None, "row", "col"),
        P("row", None, "col"),
        P(),
    )
    out_specs = P(None, "row", "col", None)
    return jax.shard_map(
        per_block, mesh=mesh, in_specs=in_specs, out_specs=out_specs, check_vma=False
    )
```

```python
import functools
import math

import jax
import jax.numpy as jnp
import numpy as np
from jax import lax
from jax.experimental import pallas as pl
from jax.experimental.pallas import tpu as pltpu
from jax.sharding import PartitionSpec as P

QUANT = 8
TAPS = 4


BETA = 0.5
HIGH = lax.Precision.HIGHEST
LANES = 128
SUBLANES = 8
MESH = pl.DeviceIdType.MESH


def with_halo(block, sides, width):
    for axis, dim in sides:
        count = lax.axis_size(axis)
        forward = [(i, i + 1) for i in range(count - 1)]
        forward.append((count - 1, 0))
        backward = [(target, source) for source, target in forward]
        low = lax.ppermute(
            lax.slice_in_dim(block, block.shape[dim] - width, None, axis=dim), axis, forward
        )
        high = lax.ppermute(lax.slice_in_dim(block, 0, width, axis=dim), axis, backward)
        block = jnp.concatenate([low, block, high], axis=dim)
    return block


def central(values, axis):
    return (jnp.roll(values, -1, axis) - jnp.roll(values, 1, axis)) * 0.5


def second_difference(values, axis):
    return 2.0 * values - jnp.roll(values, -1, axis) - jnp.roll(values, 1, axis)


def tap_weights(levels, weight):
    taps = []
    for tap in range(TAPS):
        value = jnp.zeros(levels.shape, jnp.float32)
        for level in range(QUANT):
            value = jnp.where(levels == level, weight(level, tap), value)
        taps.append(value)
    return taps


def transport(template_y, departure, weights):
    planes, lines, columns = template_y.shape
    blocks = departure.shape[1]
    span = lines // blocks
    shift_cells = jnp.floor_divide(departure, QUANT)
    levels = departure - shift_cells * QUANT
    taps = tap_weights(levels, lambda level, tap: weights[level, tap])
    shift = jnp.mod(shift_cells + 1, lines)
    parts = []
    for block in range(blocks):
        rolled = template_y
        step = 1
        while step < lines:
            chosen = (shift[:, block : block + 1] & step) != 0
            rolled = jnp.where(chosen, jnp.roll(rolled, step, 1), rolled)
            step *= 2
        part = 0.0
        for tap in range(TAPS):
            turned = jnp.roll(rolled, -tap - block * span, 1)[:, :span]
            part = part + taps[tap][:, block : block + 1] * turned
        parts.append(part)
    return jnp.concatenate(parts, axis=1)


def curvature(velocity_z):
    field_shape = velocity_z.shape
    length = field_shape[-1]
    inner = 128
    outer = length // inner
    lines = velocity_z.reshape(-1, outer, inner)
    angle = 2.0 * math.pi / length
    outer_index = jnp.arange(outer, dtype=jnp.int32)
    inner_index = jnp.arange(inner, dtype=jnp.int32)
    outer_phase = (
        jnp.mod(outer_index[:, None] * outer_index[None, :] * inner, length).astype(jnp.float32)
        * angle
    )
    cos_outer = jnp.cos(outer_phase)
    sin_outer = jnp.sin(outer_phase)
    twist_phase = (
        jnp.mod(outer_index[:, None] * inner_index[None, :], length).astype(jnp.float32) * angle
    )
    cos_twist = jnp.cos(twist_phase)
    sin_twist = jnp.sin(twist_phase)
    inner_phase = (
        jnp.mod(inner_index[:, None] * inner_index[None, :] * outer, length).astype(jnp.float32)
        * angle
    )
    cos_inner = jnp.cos(inner_phase)
    sin_inner = jnp.sin(inner_phase)
    freq_index = outer_index[:, None] + outer * inner_index[None, :]
    signed = jnp.where(freq_index < length // 2, freq_index, freq_index - length).astype(
        jnp.float32
    )
    symbol = (signed * angle) ** 2 / length
    real_one = jnp.einsum("lap,ak->lkp", lines, cos_outer, precision=HIGH)
    imag_one = -jnp.einsum("lap,ak->lkp", lines, sin_outer, precision=HIGH)
    real_two = real_one * cos_twist + imag_one * sin_twist
    imag_two = imag_one * cos_twist - real_one * sin_twist
    real_three = jnp.einsum("lkp,pq->lkq", real_two, cos_inner, precision=HIGH) + jnp.einsum(
        "lkp,pq->lkq", imag_two, sin_inner, precision=HIGH
    )
    imag_three = jnp.einsum("lkp,pq->lkq", imag_two, cos_inner, precision=HIGH) - jnp.einsum(
        "lkp,pq->lkq", real_two, sin_inner, precision=HIGH
    )
    real_three = real_three * symbol
    imag_three = imag_three * symbol
    real_four = jnp.einsum("lkq,pq->lkp", real_three, cos_inner, precision=HIGH) - jnp.einsum(
        "lkq,pq->lkp", imag_three, sin_inner, precision=HIGH
    )
    imag_four = jnp.einsum("lkq,pq->lkp", imag_three, cos_inner, precision=HIGH) + jnp.einsum(
        "lkq,pq->lkp", real_three, sin_inner, precision=HIGH
    )
    real_five = real_four * cos_twist - imag_four * sin_twist
    imag_five = imag_four * cos_twist + real_four * sin_twist
    result = jnp.einsum("lkp,kn->lnp", real_five, cos_outer, precision=HIGH) - jnp.einsum(
        "lkp,kn->lnp", imag_five, sin_outer, precision=HIGH
    )
    return result.reshape(field_shape)


def spectral(arrived):
    return (arrived, curvature(arrived[3:6]))


def per_device(template, target, velocity, departure, weights):
    across = second_difference(velocity, 1)
    bundle = jnp.concatenate([template[None], target[None], velocity, across], axis=0)
    regrouped = lax.all_to_all(bundle, "row", split_axis=1, concat_axis=2, tiled=True)
    moved_image = transport(regrouped[0], departure, weights)
    misfit = regrouped[1] - moved_image
    pull_along = misfit * central(moved_image, 1)
    velocity_y = regrouped[2:5]
    second_part = second_difference(velocity_y, 2)
    second_part = regrouped[5:8] + second_part
    outgoing = jnp.concatenate(
        [misfit[None], moved_image[None], pull_along[None], velocity_y, second_part], axis=0
    )
    columns_z, bending = spectral(
        lax.all_to_all(outgoing, "col", split_axis=2, concat_axis=3, tiled=True)
    )
    misfit_z = columns_z[0]
    moved_z = columns_z[1]
    second_z = columns_z[6:9]
    padded = with_halo(moved_z, (("row", 0),), 1)
    slope_across = (padded[2:] - padded[:-2]) * 0.5
    force = jnp.stack([misfit_z * slope_across, columns_z[2], misfit_z * central(moved_z, 2)])
    return BETA * (second_z + bending) + force


def split_halves(values):
    high = values.astype(jnp.bfloat16)
    return high, (values - high.astype(jnp.float32)).astype(jnp.bfloat16)


def dot_split(left, right):
    dot = functools.partial(jnp.dot, preferred_element_type=jnp.float32)
    return dot(left[0], right[0]) + (dot(left[0], right[1]) + dot(left[1], right[0]))


def halves_of(matrix):
    high = matrix.astype(np.float32).astype(jnp.bfloat16)
    low = (matrix - high.astype(np.float64)).astype(np.float32).astype(jnp.bfloat16)
    return np.stack([high, low])


def operators(length, rows):
    outer = length // LANES
    frequency = np.fft.fftfreq(length) * length
    response = np.real(np.fft.ifft((2.0 * math.pi / length * frequency) ** 2))
    response[0] += 4.0
    response *= BETA
    inner = np.arange(LANES)
    group = np.arange(outer)
    away = np.mod(
        LANES * group[:, None, None] + inner[None, :, None] - inner[None, None, :], length
    )
    mixed = np.fft.fft(response[away], axis=0)
    pairs = []
    forward = np.zeros((outer, outer))
    inverse = np.zeros((outer, outer))
    forward[0] = 1.0
    forward[1] = (-1.0) ** group
    inverse[:, 0] = 1.0 / outer
    inverse[:, 1] = (-1.0) ** group / outer
    zero = np.zeros((LANES, LANES))
    pairs.append(np.block([[mixed[0].real.T, zero], [zero, mixed[outer // 2].real.T]]))
    for k in range(1, outer // 2):
        real, imag = mixed[k].real.T, mixed[k].imag.T
        pairs.append(np.block([[real, imag], [-imag, real]]))
        phase = 2.0 * math.pi * k * group / outer
        forward[2 * k] = np.cos(phase)
        forward[2 * k + 1] = -np.sin(phase)
        inverse[:, 2 * k] = 2.0 * np.cos(phase) / outer
        inverse[:, 2 * k + 1] = -2.0 * np.sin(phase) / outer
    same = np.eye(rows)
    ahead = np.kron(forward, same)
    back = np.kron(inverse, same)
    return halves_of(ahead), halves_of(np.stack(pairs)), halves_of(back)


def kernel(
    extent,
    template,
    target,
    velocity,
    departure_hbm,
    weights_hbm,
    ahead_hbm,
    pairs_hbm,
    back_hbm,
    out,
    departure,
    weights,
    template_y,
    target_z,
    velocity_z,
    edge,
    extended,
    extended_edge,
    moved,
    moved_edge,
    moved_low,
    moved_high,
    slope,
    rest,
    spectrum,
    ahead,
    pairs,
    back,
    load_sem,
    send_sem,
    recv_sem,
    ready_sem,
):
    rows, columns = extent
    row, column = lax.axis_index("row"), lax.axis_index("col")
    planes, lines, slab = template_y.shape[:3]
    components = velocity_z.shape[0]
    own = lines // columns
    outer = columns * slab
    owner = row // own
    place = lax.rem(row, own)
    groups = [pl.ds(0, components - 1), pl.ds(components - 1, 1)]
    TEMPLATE, TARGET, MOVED, MOVED_EDGE, LOW, HIGH_SIDE, VELOCITY = 0, 1, 2, 3, 5, 6, 7
    SIDE_LOW, SIDE_HIGH, EDGE_LOW, EDGE_HIGH = (
        VELOCITY + i * len(groups) for i in range(1, 5)
    )
    extent_x = velocity.shape[1]
    here_z = pl.ds(pl.multiple_of(column * slab, slab), slab)

    loads = [
        pltpu.make_async_copy(source, sink, load_sem.at[i])
        for i, (source, sink) in enumerate(
            [
                (departure_hbm, departure),
                (weights_hbm, weights),
                (ahead_hbm, ahead),
                (pairs_hbm, pairs),
                (back_hbm, back),
            ]
        )
    ]

    near = own // 2
    here = lax.rem(row, near)
    line = [
        (lax.rem(row + i * near, rows), lax.rem(column + j, columns))
        for i in range(rows // near)
        for j in range(columns)
        if i + j > 0
    ]
    mates = [(row - here + lax.rem(here + i, near), column) for i in range(1, near)]
    barrier = pltpu.get_barrier_semaphore()
    for device in line + mates:
        pl.semaphore_signal(barrier, inc=1, device_id=device, device_id_type=MESH)
    for load in loads:
        load.start()
    pl.semaphore_wait(barrier, len(line) + len(mates))
    for device in mates:
        pl.semaphore_signal(ready_sem, inc=1, device_id=device, device_id_type=MESH)

    def remote(source, sink, kind, to):
        return pltpu.make_async_remote_copy(
            src_ref=source,
            dst_ref=sink,
            send_sem=send_sem.at[kind],
            recv_sem=recv_sem.at[kind],
            device_id=to,
            device_id_type=MESH,
        )

    def deliver(source, sink, kind, to, stays=None):
        def go():
            remote(source, sink, kind, to).start()

        if stays is None:
            go()
            return
        pl.when(jnp.logical_not(stays))(go)

        @pl.when(stays)
        def _():
            pltpu.make_async_copy(source, sink, recv_sem.at[kind]).start()

    def sent(ref, kind):
        pltpu.make_async_copy(ref, ref, send_sem.at[kind]).wait()

    def arrived(ref, kind):
        pltpu.make_async_copy(ref, ref, recv_sem.at[kind]).wait()

    inside = owner == column
    def turned(spot):
        return spot // 2 + spot % 2 * (near // 2)

    skipped = here // (near // 2) + here % (near // 2) * 2
    early, front, back_rows = [], [], []
    for d in [*range(1, columns), 0]:
        base = lax.rem(owner + d, columns) * own
        for quad, group in ((0, front), (near, back_rows)):
            if d > 0:
                early.append((False, base + quad + here))
                for k in range(near - 1):
                    after = jnp.where(k >= skipped, turned(k + 1), turned(k))
                    group.append((False, base + quad + after))
            else:
                for k in range(near):
                    group.append((True, base + quad + turned(k)))
    others = front + back_rows

    def apart(rows_of):
        return [(mine, to) for mine, to in rows_of if not mine]

    def within(rows_of):
        return [(mine, to) for mine, to in rows_of if mine]

    def send_template(rows_of):
        for mine, to in rows_of:
            source = template.at[pl.ds(to * planes, planes)]
            sink = template_y.at[:, row]
            deliver(source, sink, TEMPLATE, (to, column), row == to if mine else None)

    def send_target(rows_of):
        for mine, to in rows_of:
            deliver(
                target.at[pl.ds(to * planes, planes)],
                target_z.at[:, here_z, place],
                TARGET,
                (to, owner),
                jnp.logical_and(inside, row == to) if mine else None,
            )

    def send_velocity(group, rows_of):
        comps = groups[group]
        for mine, to in rows_of:
            deliver(
                velocity.at[comps, pl.ds(to * planes, planes)],
                velocity_z.at[comps, pl.ds(1, planes), here_z, place],
                VELOCITY + group,
                (to, owner),
                jnp.logical_and(inside, row == to) if mine else None,
            )

    def send_halo(group):
        comps = groups[group]
        for h in range(columns):
            for to, plane, at in (
                (h * own, (h * own * planes - 1) % extent_x, 0),
                (h * own + own - 1, (h + 1) * own * planes % extent_x, planes + 1),
            ):
                deliver(
                    velocity.at[comps, plane],
                    velocity_z.at[comps, at, here_z, place],
                    VELOCITY + group,
                    (to, owner),
                    jnp.logical_and(inside, row == to),
                )

    def beside(group, go):
        comps = groups[group]
        mine = pl.ds(1, planes)
        go(
            velocity_z.at[comps, mine, :, own - 1],
            edge.at[comps, :, :, 0],
            EDGE_LOW + group,
            (row, lax.rem(column + 1, columns)),
        )
        go(
            velocity_z.at[comps, mine, :, 0],
            edge.at[comps, :, :, 1],
            EDGE_HIGH + group,
            (row, lax.rem(column + columns - 1, columns)),
        )

        @pl.when(place < own - 1)
        def _():
            go(
                velocity_z.at[comps, planes],
                velocity_z.at[comps, 0],
                SIDE_LOW + group,
                (lax.rem(row + 1, rows), column),
            )

        @pl.when(place > 0)
        def _():
            go(
                velocity_z.at[comps, 1],
                velocity_z.at[comps, planes + 1],
                SIDE_HIGH + group,
                (lax.rem(row + rows - 1, rows), column),
            )

    def beside_sent(*copy):
        remote(*copy).wait_send()

    def velocity_sent(group):
        comps = groups[group]
        ends = jnp.logical_or(place == 0, place == own - 1)
        kept = jnp.logical_and(inside, ends)
        total = planes * rows

        @pl.when(inside)
        def _():
            sent(velocity.at[comps, pl.ds(0, total - planes)], VELOCITY + group)

        @pl.when(jnp.logical_not(inside))
        def _():
            sent(velocity.at[comps, pl.ds(0, total)], VELOCITY + group)

        @pl.when(kept)
        def _():
            sent(velocity.at[comps, pl.ds(0, 2 * columns - 1)], VELOCITY + group)

        @pl.when(jnp.logical_not(kept))
        def _():
            sent(velocity.at[comps, pl.ds(0, 2 * columns)], VELOCITY + group)

    def target_sent():
        total = planes * rows

        @pl.when(inside)
        def _():
            sent(target.at[pl.ds(0, total - planes)], TARGET)

        @pl.when(jnp.logical_not(inside))
        def _():
            sent(target.at[pl.ds(0, total)], TARGET)

    def moved_sent():
        for _ in range(columns - 1):
            sent(extended.at[:, 0], MOVED)
            for r in range(2):
                sent(extended_edge.at[:, 0, :, r], MOVED_EDGE + r)
        sent(extended.at[0], LOW)
        sent(extended.at[0], HIGH_SIDE)

    def transport_lines():
        blocks = departure.shape[1]
        span = lines // blocks
        for plane in range(planes):
            image = [template_y[plane, y] for y in range(lines)]
            values = []
            for block in range(blocks):
                offset = departure[plane, block]
                whole = offset >> (QUANT.bit_length() - 1)
                levels = offset - whole * QUANT
                taps = tap_weights(levels, lambda level, tap: weights[tap, level])
                shift = jnp.where(whole + 1 < 0, whole + 1 + lines, whole + 1)
                rolled = image
                step = 1
                while step < lines:
                    chosen = (shift & step) != 0
                    rolled = [
                        jnp.where(chosen, rolled[(y - step) % lines], rolled[y])
                        for y in range(lines)
                    ]
                    step *= 2
                for y in range(block * span, (block + 1) * span):
                    value = taps[0] * rolled[y]
                    for tap in range(1, TAPS):
                        value = value + taps[tap] * rolled[(y + tap) % lines]
                    values.append(value)
            for y in range(lines):
                extended[plane, y // own, :, y % own, :] = values[y]
            for j in range(columns):
                extended_edge[plane, j, :, 0, :] = values[(j * own - 1) % lines]
                extended_edge[plane, j, :, 1, :] = values[(j * own + own) % lines]

    def send_moved():
        up, down = lax.rem(row + 1, rows), lax.rem(row + rows - 1, rows)
        for j in range(columns):
            to = lax.rem(column + j, columns)
            deliver(extended.at[planes - 1, to], moved_low.at[here_z], LOW, (up, to))
            deliver(extended.at[0, to], moved_high.at[here_z], HIGH_SIDE, (down, to))
            if j > 0:
                deliver(extended.at[:, to], moved.at[:, here_z], MOVED, (row, to))
                for r in range(2):
                    deliver(
                        extended_edge.at[:, to, :, r],
                        moved_edge.at[:, here_z, r],
                        MOVED_EDGE + r,
                        (row, to),
                    )
    def velocity_arrived(group):
        comps = groups[group]

        @pl.when(place == 0)
        def _():
            arrived(velocity_z.at[comps, pl.ds(0, planes + 1)], VELOCITY + group)

        @pl.when(place == own - 1)
        def _():
            arrived(velocity_z.at[comps, pl.ds(1, planes + 1)], VELOCITY + group)

        @pl.when(place * (own - 1 - place) > 0)
        def _():
            arrived(velocity_z.at[comps, pl.ds(1, planes)], VELOCITY + group)

    def beside_arrived(group):
        comps = groups[group]
        arrived(edge.at[comps, :, :, 0], EDGE_LOW + group)
        arrived(edge.at[comps, :, :, 1], EDGE_HIGH + group)

        @pl.when(place > 0)
        def _():
            arrived(velocity_z.at[comps, 0], SIDE_LOW + group)

        @pl.when(place < own - 1)
        def _():
            arrived(velocity_z.at[comps, planes + 1], SIDE_HIGH + group)

    def moved_arrived():
        for _ in range(columns - 1):
            arrived(moved.at[:, pl.ds(0, slab)], MOVED)
            for r in range(2):
                arrived(moved_edge.at[:, pl.ds(0, slab), r], MOVED_EDGE + r)
        arrived(moved_low, LOW)
        arrived(moved_high, HIGH_SIDE)

    def in_lines(values, low, high):
        after = jnp.concatenate([values[:, 1:], high], axis=1)
        before = jnp.concatenate([low, values[:, :-1]], axis=1)
        return before, after

    def slopes():
        lane = lax.broadcasted_iota(jnp.int32, (outer, own, LANES), 2)
        for plane in range(planes):
            here = moved[plane]
            below = moved[plane - 1] if plane > 0 else moved_low[...]
            above = moved[plane + 1] if plane < planes - 1 else moved_high[...]
            slope[0, plane] = 0.5 * (above - below)
            before, after = in_lines(
                here, moved_edge[plane, :, 0:1], moved_edge[plane, :, 1:2]
            )
            slope[1, plane] = 0.5 * (after - before)
            following = jnp.roll(here, -1, 2)
            following = jnp.where(lane == LANES - 1, jnp.roll(following, -1, 0), following)
            previous = jnp.roll(here, 1, 2)
            previous = jnp.where(lane == 0, jnp.roll(previous, 1, 0), previous)
            slope[2, plane] = 0.5 * (following - previous)

    def to_spectrum(group):
        ahead_parts = (ahead[0], ahead[1])
        comps = groups[group]
        for comp in range(comps.start, comps.start + comps.size):
            for plane in range(planes):
                block = velocity_z[comp, plane + 1].reshape(outer * own, LANES)
                spectrum[:, comp, plane] = dot_split(ahead_parts, split_halves(block)).reshape(
                    outer, own, LANES
                )

    def respond():
        for pair in range(outer // 2):
            shape = (components * planes * own, LANES)
            joined = jnp.concatenate(
                [spectrum[2 * pair].reshape(shape), spectrum[2 * pair + 1].reshape(shape)], axis=1
            )
            result = dot_split(split_halves(joined), (pairs[0, pair], pairs[1, pair]))
            shape = (components, planes, own, LANES)
            spectrum[2 * pair] = result[:, :LANES].reshape(shape)
            spectrum[2 * pair + 1] = result[:, LANES:].reshape(shape)

    def from_spectrum():
        back_parts = (back[0], back[1])
        for comp in range(components):
            for plane in range(planes):
                block = spectrum[:, comp, plane].reshape(outer * own, LANES)
                result = dot_split(back_parts, split_halves(block))
                rest[comp, plane] = result.reshape(outer, own, LANES)

    def add_sides(group):
        comps = groups[group]
        for comp in range(comps.start, comps.start + comps.size):
            for plane in range(planes):
                before, after = in_lines(
                    velocity_z[comp, plane + 1],
                    edge[comp, plane, :, 0:1],
                    edge[comp, plane, :, 1:2],
                )
                sides = (velocity_z[comp, plane] + velocity_z[comp, plane + 2]) + (before + after)
                rest[comp, plane] -= BETA * sides

    send_template(early)
    send_velocity(0, early)
    pl.semaphore_wait(ready_sem, len(mates))
    send_template(apart(others) + within(others))
    send_halo(0)
    send_velocity(1, early)
    send_halo(1)
    for half in (front, back_rows):
        for part in (apart(half), within(half)):
            for group in range(len(groups)):
                send_velocity(group, part)
    for load in loads:
        load.wait()
    arrived(template_y, TEMPLATE)
    transport_lines()
    send_moved()
    moved[:, here_z] = extended[:, column]
    moved_edge[:, here_z] = extended_edge[:, column]
    send_target(early)
    send_target(apart(others) + within(others))
    for group in range(len(groups)):
        velocity_arrived(group)
        beside(group, deliver)
        to_spectrum(group)
    respond()
    moved_arrived()
    slopes()
    from_spectrum()
    sent(template_y.at[:, pl.ds(0, rows - 1)], TEMPLATE)
    moved_sent()
    for group in range(len(groups)):
        velocity_sent(group)
        beside_arrived(group)
        add_sides(group)
        beside(group, beside_sent)
    arrived(target_z, TARGET)
    for plane in range(planes):
        misfit = target_z[plane] - moved[plane]
        for comp in range(components):
            total = rest[comp, plane] + misfit * slope[comp, plane]
            for tile in range(outer):
                out[comp, plane, :, tile * LANES : (tile + 1) * LANES] = total[tile]
    target_sent()


def direct(template, target, velocity, departure, weights):
    rows, columns = lax.axis_size("row"), lax.axis_size("col")
    extent_x, _, cells = template.shape
    components = velocity.shape[0]
    planes = extent_x // rows
    lines = rows
    own = lines // columns
    slab = cells // LANES
    outer = slab * columns
    ahead, pairs, back = operators(cells * columns, own)
    tile = (slab, LANES)
    whole = (outer, own, LANES)
    hbm = pl.BlockSpec(memory_space=pl.ANY)
    vmem = pl.BlockSpec(memory_space=pltpu.VMEM)
    kinds = 7 + 5 * 2
    return pl.pallas_call(
        functools.partial(kernel, (rows, columns)),
        out_shape=pltpu.VMEM((components, planes, own, outer * LANES), jnp.float32),
        in_specs=[hbm] * 8,
        out_specs=vmem,
        scratch_shapes=[
            pltpu.VMEM(departure.shape[:2] + tile, jnp.int32),
            pltpu.SMEM(weights.shape[::-1], jnp.float32),
            pltpu.VMEM((planes, lines) + tile, jnp.float32),
            pltpu.VMEM((planes,) + whole, jnp.float32),
            pltpu.VMEM((components, planes + 2) + whole, jnp.float32),
            pltpu.VMEM((components, planes, outer, SUBLANES, LANES), jnp.float32),
            pltpu.VMEM((planes, columns, slab, own, LANES), jnp.float32),
            pltpu.VMEM((planes, columns, slab, SUBLANES, LANES), jnp.float32),
            pltpu.VMEM((planes,) + whole, jnp.float32),
            pltpu.VMEM((planes, outer, SUBLANES, LANES), jnp.float32),
            pltpu.VMEM(whole, jnp.float32),
            pltpu.VMEM(whole, jnp.float32),
            pltpu.VMEM((components, planes) + whole, jnp.float32),
            pltpu.VMEM((components, planes) + whole, jnp.float32),
            pltpu.VMEM((outer, components, planes, own, LANES), jnp.float32),
            pltpu.VMEM(ahead.shape, jnp.bfloat16),
            pltpu.VMEM(pairs.shape, jnp.bfloat16),
            pltpu.VMEM(back.shape, jnp.bfloat16),
            pltpu.SemaphoreType.DMA((5,)),
            pltpu.SemaphoreType.DMA((kinds,)),
            pltpu.SemaphoreType.DMA((kinds,)),
            pltpu.SemaphoreType.REGULAR,
        ],
        compiler_params=pltpu.CompilerParams(collective_id=0, has_side_effects=True),
    )(
        template.reshape((extent_x,) + tile),
        target.reshape((extent_x,) + tile),
        velocity.reshape((components, extent_x) + tile),
        departure.reshape(departure.shape[:2] + tile),
        weights.T,
        jnp.asarray(ahead),
        jnp.asarray(pairs),
        jnp.asarray(back),
    )


def per_block(template, target, velocity, departure, weights):
    rows, columns = lax.axis_size("row"), lax.axis_size("col")
    components = velocity.shape[0]
    one_line = template.shape[1] == 1 and rows % columns == 0 and columns > 1 and components > 1
    whole_tiles = template.shape[2] % (LANES * SUBLANES) == 0
    short = rows // columns == SUBLANES and template.shape[0] % rows == 0
    if one_line and whole_tiles and short:
        return direct(template, target, velocity, departure, weights)
    return per_device(template, target, velocity, departure, weights)


def solution(mesh):
    in_specs = (
        P(None, "row", "col"),
        P(None, "row", "col"),
        P(None, None, "row", "col"),
        P("row", None, "col"),
        P(),
    )
    out_specs = P(None, "row", "col", None)
    return jax.shard_map(
        per_block, mesh=mesh, in_specs=in_specs, out_specs=out_specs, check_vma=False
    )
```

```python
import functools
import math

import jax
import jax.numpy as jnp
import numpy as np
from jax import lax
from jax.experimental import pallas as pl
from jax.experimental.pallas import tpu as pltpu
from jax.sharding import PartitionSpec as P

QUANT = 8
TAPS = 4


BETA = 0.5
HIGH = lax.Precision.HIGHEST
LANES = 128
SUBLANES = 8
MESH = pl.DeviceIdType.MESH


def with_halo(block, sides, width):
    for axis, dim in sides:
        count = lax.axis_size(axis)
        forward = [(i, i + 1) for i in range(count - 1)]
        forward.append((count - 1, 0))
        backward = [(target, source) for source, target in forward]
        low = lax.ppermute(
            lax.slice_in_dim(block, block.shape[dim] - width, None, axis=dim), axis, forward
        )
        high = lax.ppermute(lax.slice_in_dim(block, 0, width, axis=dim), axis, backward)
        block = jnp.concatenate([low, block, high], axis=dim)
    return block


def central(values, axis):
    return (jnp.roll(values, -1, axis) - jnp.roll(values, 1, axis)) * 0.5


def second_difference(values, axis):
    return 2.0 * values - jnp.roll(values, -1, axis) - jnp.roll(values, 1, axis)


def tap_weights(levels, weight):
    taps = []
    for tap in range(TAPS):
        value = jnp.zeros(levels.shape, jnp.float32)
        for level in range(QUANT):
            value = jnp.where(levels == level, weight(level, tap), value)
        taps.append(value)
    return taps


def transport(template_y, departure, weights):
    planes, lines, columns = template_y.shape
    blocks = departure.shape[1]
    span = lines // blocks
    shift_cells = jnp.floor_divide(departure, QUANT)
    levels = departure - shift_cells * QUANT
    taps = tap_weights(levels, lambda level, tap: weights[level, tap])
    shift = jnp.mod(shift_cells + 1, lines)
    parts = []
    for block in range(blocks):
        rolled = template_y
        step = 1
        while step < lines:
            chosen = (shift[:, block : block + 1] & step) != 0
            rolled = jnp.where(chosen, jnp.roll(rolled, step, 1), rolled)
            step *= 2
        part = 0.0
        for tap in range(TAPS):
            turned = jnp.roll(rolled, -tap - block * span, 1)[:, :span]
            part = part + taps[tap][:, block : block + 1] * turned
        parts.append(part)
    return jnp.concatenate(parts, axis=1)


def curvature(velocity_z):
    field_shape = velocity_z.shape
    length = field_shape[-1]
    inner = 128
    outer = length // inner
    lines = velocity_z.reshape(-1, outer, inner)
    angle = 2.0 * math.pi / length
    outer_index = jnp.arange(outer, dtype=jnp.int32)
    inner_index = jnp.arange(inner, dtype=jnp.int32)
    outer_phase = (
        jnp.mod(outer_index[:, None] * outer_index[None, :] * inner, length).astype(jnp.float32)
        * angle
    )
    cos_outer = jnp.cos(outer_phase)
    sin_outer = jnp.sin(outer_phase)
    twist_phase = (
        jnp.mod(outer_index[:, None] * inner_index[None, :], length).astype(jnp.float32) * angle
    )
    cos_twist = jnp.cos(twist_phase)
    sin_twist = jnp.sin(twist_phase)
    inner_phase = (
        jnp.mod(inner_index[:, None] * inner_index[None, :] * outer, length).astype(jnp.float32)
        * angle
    )
    cos_inner = jnp.cos(inner_phase)
    sin_inner = jnp.sin(inner_phase)
    freq_index = outer_index[:, None] + outer * inner_index[None, :]
    signed = jnp.where(freq_index < length // 2, freq_index, freq_index - length).astype(
        jnp.float32
    )
    symbol = (signed * angle) ** 2 / length
    real_one = jnp.einsum("lap,ak->lkp", lines, cos_outer, precision=HIGH)
    imag_one = -jnp.einsum("lap,ak->lkp", lines, sin_outer, precision=HIGH)
    real_two = real_one * cos_twist + imag_one * sin_twist
    imag_two = imag_one * cos_twist - real_one * sin_twist
    real_three = jnp.einsum("lkp,pq->lkq", real_two, cos_inner, precision=HIGH) + jnp.einsum(
        "lkp,pq->lkq", imag_two, sin_inner, precision=HIGH
    )
    imag_three = jnp.einsum("lkp,pq->lkq", imag_two, cos_inner, precision=HIGH) - jnp.einsum(
        "lkp,pq->lkq", real_two, sin_inner, precision=HIGH
    )
    real_three = real_three * symbol
    imag_three = imag_three * symbol
    real_four = jnp.einsum("lkq,pq->lkp", real_three, cos_inner, precision=HIGH) - jnp.einsum(
        "lkq,pq->lkp", imag_three, sin_inner, precision=HIGH
    )
    imag_four = jnp.einsum("lkq,pq->lkp", imag_three, cos_inner, precision=HIGH) + jnp.einsum(
        "lkq,pq->lkp", real_three, sin_inner, precision=HIGH
    )
    real_five = real_four * cos_twist - imag_four * sin_twist
    imag_five = imag_four * cos_twist + real_four * sin_twist
    result = jnp.einsum("lkp,kn->lnp", real_five, cos_outer, precision=HIGH) - jnp.einsum(
        "lkp,kn->lnp", imag_five, sin_outer, precision=HIGH
    )
    return result.reshape(field_shape)


def spectral(arrived):
    return (arrived, curvature(arrived[3:6]))


def per_device(template, target, velocity, departure, weights):
    across = second_difference(velocity, 1)
    bundle = jnp.concatenate([template[None], target[None], velocity, across], axis=0)
    regrouped = lax.all_to_all(bundle, "row", split_axis=1, concat_axis=2, tiled=True)
    moved_image = transport(regrouped[0], departure, weights)
    misfit = regrouped[1] - moved_image
    pull_along = misfit * central(moved_image, 1)
    velocity_y = regrouped[2:5]
    second_part = second_difference(velocity_y, 2)
    second_part = regrouped[5:8] + second_part
    outgoing = jnp.concatenate(
        [misfit[None], moved_image[None], pull_along[None], velocity_y, second_part], axis=0
    )
    columns_z, bending = spectral(
        lax.all_to_all(outgoing, "col", split_axis=2, concat_axis=3, tiled=True)
    )
    misfit_z = columns_z[0]
    moved_z = columns_z[1]
    second_z = columns_z[6:9]
    padded = with_halo(moved_z, (("row", 0),), 1)
    slope_across = (padded[2:] - padded[:-2]) * 0.5
    force = jnp.stack([misfit_z * slope_across, columns_z[2], misfit_z * central(moved_z, 2)])
    return BETA * (second_z + bending) + force


def split_halves(values):
    high = values.astype(jnp.bfloat16)
    return high, (values - high.astype(jnp.float32)).astype(jnp.bfloat16)


def dot_split(left, right):
    dot = functools.partial(jnp.dot, preferred_element_type=jnp.float32)
    return dot(left[0], right[0]) + (dot(left[0], right[1]) + dot(left[1], right[0]))


def halves_of(matrix):
    high = matrix.astype(np.float32).astype(jnp.bfloat16)
    low = (matrix - high.astype(np.float64)).astype(np.float32).astype(jnp.bfloat16)
    return np.stack([high, low])


def operators(length, rows):
    outer = length // LANES
    frequency = np.fft.fftfreq(length) * length
    response = np.real(np.fft.ifft((2.0 * math.pi / length * frequency) ** 2))
    response[0] += 4.0
    response *= BETA
    inner = np.arange(LANES)
    group = np.arange(outer)
    away = np.mod(
        LANES * group[:, None, None] + inner[None, :, None] - inner[None, None, :], length
    )
    mixed = np.fft.fft(response[away], axis=0)
    pairs = []
    forward = np.zeros((outer, outer))
    inverse = np.zeros((outer, outer))
    forward[0] = 1.0
    forward[1] = (-1.0) ** group
    inverse[:, 0] = 1.0 / outer
    inverse[:, 1] = (-1.0) ** group / outer
    zero = np.zeros((LANES, LANES))
    pairs.append(np.block([[mixed[0].real.T, zero], [zero, mixed[outer // 2].real.T]]))
    for k in range(1, outer // 2):
        real, imag = mixed[k].real.T, mixed[k].imag.T
        pairs.append(np.block([[real, imag], [-imag, real]]))
        phase = 2.0 * math.pi * k * group / outer
        forward[2 * k] = np.cos(phase)
        forward[2 * k + 1] = -np.sin(phase)
        inverse[:, 2 * k] = 2.0 * np.cos(phase) / outer
        inverse[:, 2 * k + 1] = -2.0 * np.sin(phase) / outer
    same = np.eye(rows)
    ahead = np.kron(forward, same)
    back = np.kron(inverse, same)
    return halves_of(ahead), halves_of(np.stack(pairs)), halves_of(back)


def kernel(
    extent,
    template,
    target,
    velocity,
    departure_hbm,
    weights_hbm,
    ahead_hbm,
    pairs_hbm,
    back_hbm,
    out,
    departure,
    weights,
    template_y,
    target_z,
    velocity_z,
    edge,
    extended,
    extended_edge,
    moved,
    moved_edge,
    moved_low,
    moved_high,
    slope,
    rest,
    spectrum,
    ahead,
    pairs,
    back,
    load_sem,
    send_sem,
    recv_sem,
    ready_sem,
):
    rows, columns = extent
    row, column = lax.axis_index("row"), lax.axis_index("col")
    planes, lines, slab = template_y.shape[:3]
    components = velocity_z.shape[0]
    own = lines // columns
    outer = columns * slab
    owner = row // own
    place = lax.rem(row, own)
    groups = [pl.ds(0, components - 1), pl.ds(components - 1, 1)]
    TEMPLATE, TARGET, MOVED, MOVED_EDGE, LOW, HIGH_SIDE, VELOCITY = 0, 1, 2, 3, 5, 6, 7
    SIDE_LOW, SIDE_HIGH, EDGE_LOW, EDGE_HIGH = (
        VELOCITY + i * len(groups) for i in range(1, 5)
    )
    extent_x = velocity.shape[1]
    here_z = pl.ds(pl.multiple_of(column * slab, slab), slab)

    loads = [
        pltpu.make_async_copy(source, sink, load_sem.at[i])
        for i, (source, sink) in enumerate(
            [
                (departure_hbm, departure),
                (weights_hbm, weights),
                (ahead_hbm, ahead),
                (pairs_hbm, pairs),
                (back_hbm, back),
            ]
        )
    ]

    near = own // 2
    here = lax.rem(row, near)
    line = [
        (lax.rem(row + i * near, rows), lax.rem(column + j, columns))
        for i in range(rows // near)
        for j in range(columns)
        if i + j > 0
    ]
    mates = [(row - here + lax.rem(here + i, near), column) for i in range(1, near)]
    barrier = pltpu.get_barrier_semaphore()
    for device in line + mates:
        pl.semaphore_signal(barrier, inc=1, device_id=device, device_id_type=MESH)
    for load in loads:
        load.start()
    pl.semaphore_wait(barrier, len(line) + len(mates))
    for device in mates:
        pl.semaphore_signal(ready_sem, inc=1, device_id=device, device_id_type=MESH)

    def remote(source, sink, kind, to):
        return pltpu.make_async_remote_copy(
            src_ref=source,
            dst_ref=sink,
            send_sem=send_sem.at[kind],
            recv_sem=recv_sem.at[kind],
            device_id=to,
            device_id_type=MESH,
        )

    def deliver(source, sink, kind, to, stays=None):
        def go():
            remote(source, sink, kind, to).start()

        if stays is None:
            go()
            return
        pl.when(jnp.logical_not(stays))(go)

        @pl.when(stays)
        def _():
            pltpu.make_async_copy(source, sink, recv_sem.at[kind]).start()

    def sent(ref, kind):
        pltpu.make_async_copy(ref, ref, send_sem.at[kind]).wait()

    def arrived(ref, kind):
        pltpu.make_async_copy(ref, ref, recv_sem.at[kind]).wait()

    inside = owner == column
    def turned(spot):
        return spot // 2 + spot % 2 * (near // 2)

    skipped = here // (near // 2) + here % (near // 2) * 2
    early, front, back_rows = [], [], []
    for d in [*range(1, columns), 0]:
        base = lax.rem(owner + d, columns) * own
        for quad, group in ((0, front), (near, back_rows)):
            if d > 0:
                early.append((False, base + quad + here))
                for k in range(near - 1):
                    after = jnp.where(k >= skipped, turned(k + 1), turned(k))
                    group.append((False, base + quad + after))
            else:
                for k in range(near):
                    group.append((True, base + quad + turned(k)))
    others = front + back_rows

    def apart(rows_of):
        return [(mine, to) for mine, to in rows_of if not mine]

    def within(rows_of):
        return [(mine, to) for mine, to in rows_of if mine]

    def send_template(rows_of):
        for mine, to in rows_of:
            source = template.at[pl.ds(to * planes, planes)]
            sink = template_y.at[:, row]
            deliver(source, sink, TEMPLATE, (to, column), row == to if mine else None)

    def send_target(rows_of):
        for mine, to in rows_of:
            deliver(
                target.at[pl.ds(to * planes, planes)],
                target_z.at[:, here_z, place],
                TARGET,
                (to, owner),
                jnp.logical_and(inside, row == to) if mine else None,
            )

    def send_velocity(group, rows_of):
        comps = groups[group]
        for mine, to in rows_of:
            deliver(
                velocity.at[comps, pl.ds(to * planes, planes)],
                velocity_z.at[comps, pl.ds(1, planes), here_z, place],
                VELOCITY + group,
                (to, owner),
                jnp.logical_and(inside, row == to) if mine else None,
            )

    def send_halo(group):
        comps = groups[group]
        for h in range(columns):
            for to, plane, at in (
                (h * own, (h * own * planes - 1) % extent_x, 0),
                (h * own + own - 1, (h + 1) * own * planes % extent_x, planes + 1),
            ):
                deliver(
                    velocity.at[comps, plane],
                    velocity_z.at[comps, at, here_z, place],
                    VELOCITY + group,
                    (to, owner),
                    jnp.logical_and(inside, row == to),
                )

    def beside(group, go):
        comps = groups[group]
        mine = pl.ds(1, planes)
        @pl.when(place < own - 1)
        def _():
            go(
                velocity_z.at[comps, planes],
                velocity_z.at[comps, 0],
                SIDE_LOW + group,
                (lax.rem(row + 1, rows), column),
            )

        @pl.when(place > 0)
        def _():
            go(
                velocity_z.at[comps, 1],
                velocity_z.at[comps, planes + 1],
                SIDE_HIGH + group,
                (lax.rem(row + rows - 1, rows), column),
            )

        go(
            velocity_z.at[comps, mine, :, own - 1],
            edge.at[comps, :, :, 0],
            EDGE_LOW + group,
            (row, lax.rem(column + 1, columns)),
        )
        go(
            velocity_z.at[comps, mine, :, 0],
            edge.at[comps, :, :, 1],
            EDGE_HIGH + group,
            (row, lax.rem(column + columns - 1, columns)),
        )

    def beside_sent(*copy):
        remote(*copy).wait_send()

    def velocity_sent(group):
        comps = groups[group]
        ends = jnp.logical_or(place == 0, place == own - 1)
        kept = jnp.logical_and(inside, ends)
        total = planes * rows

        @pl.when(inside)
        def _():
            sent(velocity.at[comps, pl.ds(0, total - planes)], VELOCITY + group)

        @pl.when(jnp.logical_not(inside))
        def _():
            sent(velocity.at[comps, pl.ds(0, total)], VELOCITY + group)

        @pl.when(kept)
        def _():
            sent(velocity.at[comps, pl.ds(0, 2 * columns - 1)], VELOCITY + group)

        @pl.when(jnp.logical_not(kept))
        def _():
            sent(velocity.at[comps, pl.ds(0, 2 * columns)], VELOCITY + group)

    def target_sent():
        total = planes * rows

        @pl.when(inside)
        def _():
            sent(target.at[pl.ds(0, total - planes)], TARGET)

        @pl.when(jnp.logical_not(inside))
        def _():
            sent(target.at[pl.ds(0, total)], TARGET)

    def moved_sent():
        for _ in range(columns - 1):
            sent(extended.at[:, 0], MOVED)
            for r in range(2):
                sent(extended_edge.at[:, 0, :, r], MOVED_EDGE + r)
        sent(extended.at[0], LOW)
        sent(extended.at[0], HIGH_SIDE)

    def transport_lines():
        blocks = departure.shape[1]
        span = lines // blocks
        for plane in range(planes):
            image = [template_y[plane, y] for y in range(lines)]
            values = []
            for block in range(blocks):
                offset = departure[plane, block]
                whole = offset >> (QUANT.bit_length() - 1)
                levels = offset - whole * QUANT
                taps = tap_weights(levels, lambda level, tap: weights[tap, level])
                shift = jnp.where(whole + 1 < 0, whole + 1 + lines, whole + 1)
                rolled = image
                step = 1
                while step < lines:
                    chosen = (shift & step) != 0
                    rolled = [
                        jnp.where(chosen, rolled[(y - step) % lines], rolled[y])
                        for y in range(lines)
                    ]
                    step *= 2
                for y in range(block * span, (block + 1) * span):
                    value = taps[0] * rolled[y]
                    for tap in range(1, TAPS):
                        value = value + taps[tap] * rolled[(y + tap) % lines]
                    values.append(value)
            for y in range(lines):
                extended[plane, y // own, :, y % own, :] = values[y]
            for j in range(columns):
                extended_edge[plane, j, :, 0, :] = values[(j * own - 1) % lines]
                extended_edge[plane, j, :, 1, :] = values[(j * own + own) % lines]

    def send_moved():
        up, down = lax.rem(row + 1, rows), lax.rem(row + rows - 1, rows)
        for j in range(columns):
            to = lax.rem(column + j, columns)
            deliver(extended.at[planes - 1, to], moved_low.at[here_z], LOW, (up, to))
            deliver(extended.at[0, to], moved_high.at[here_z], HIGH_SIDE, (down, to))
            if j > 0:
                deliver(extended.at[:, to], moved.at[:, here_z], MOVED, (row, to))
                for r in range(2):
                    deliver(
                        extended_edge.at[:, to, :, r],
                        moved_edge.at[:, here_z, r],
                        MOVED_EDGE + r,
                        (row, to),
                    )
    def velocity_arrived(group):
        comps = groups[group]

        @pl.when(place == 0)
        def _():
            arrived(velocity_z.at[comps, pl.ds(0, planes + 1)], VELOCITY + group)

        @pl.when(place == own - 1)
        def _():
            arrived(velocity_z.at[comps, pl.ds(1, planes + 1)], VELOCITY + group)

        @pl.when(place * (own - 1 - place) > 0)
        def _():
            arrived(velocity_z.at[comps, pl.ds(1, planes)], VELOCITY + group)

    def beside_arrived(group):
        comps = groups[group]
        arrived(edge.at[comps, :, :, 0], EDGE_LOW + group)
        arrived(edge.at[comps, :, :, 1], EDGE_HIGH + group)

        @pl.when(place > 0)
        def _():
            arrived(velocity_z.at[comps, 0], SIDE_LOW + group)

        @pl.when(place < own - 1)
        def _():
            arrived(velocity_z.at[comps, planes + 1], SIDE_HIGH + group)

    def moved_arrived():
        for _ in range(columns - 1):
            arrived(moved.at[:, pl.ds(0, slab)], MOVED)
            for r in range(2):
                arrived(moved_edge.at[:, pl.ds(0, slab), r], MOVED_EDGE + r)
        arrived(moved_low, LOW)
        arrived(moved_high, HIGH_SIDE)

    def in_lines(values, low, high):
        after = jnp.concatenate([values[:, 1:], high], axis=1)
        before = jnp.concatenate([low, values[:, :-1]], axis=1)
        return before, after

    def slopes():
        lane = lax.broadcasted_iota(jnp.int32, (outer, own, LANES), 2)
        for plane in range(planes):
            here = moved[plane]
            below = moved[plane - 1] if plane > 0 else moved_low[...]
            above = moved[plane + 1] if plane < planes - 1 else moved_high[...]
            slope[0, plane] = 0.5 * (above - below)
            before, after = in_lines(
                here, moved_edge[plane, :, 0:1], moved_edge[plane, :, 1:2]
            )
            slope[1, plane] = 0.5 * (after - before)
            following = jnp.roll(here, -1, 2)
            following = jnp.where(lane == LANES - 1, jnp.roll(following, -1, 0), following)
            previous = jnp.roll(here, 1, 2)
            previous = jnp.where(lane == 0, jnp.roll(previous, 1, 0), previous)
            slope[2, plane] = 0.5 * (following - previous)

    def to_spectrum(group):
        ahead_parts = (ahead[0], ahead[1])
        comps = groups[group]
        for comp in range(comps.start, comps.start + comps.size):
            for plane in range(planes):
                block = velocity_z[comp, plane + 1].reshape(outer * own, LANES)
                spectrum[:, comp, plane] = dot_split(ahead_parts, split_halves(block)).reshape(
                    outer, own, LANES
                )

    def respond():
        for pair in range(outer // 2):
            shape = (components * planes * own, LANES)
            joined = jnp.concatenate(
                [spectrum[2 * pair].reshape(shape), spectrum[2 * pair + 1].reshape(shape)], axis=1
            )
            result = dot_split(split_halves(joined), (pairs[0, pair], pairs[1, pair]))
            shape = (components, planes, own, LANES)
            spectrum[2 * pair] = result[:, :LANES].reshape(shape)
            spectrum[2 * pair + 1] = result[:, LANES:].reshape(shape)

    def from_spectrum():
        back_parts = (back[0], back[1])
        for comp in range(components):
            for plane in range(planes):
                block = spectrum[:, comp, plane].reshape(outer * own, LANES)
                result = dot_split(back_parts, split_halves(block))
                rest[comp, plane] = result.reshape(outer, own, LANES)

    def add_sides(group):
        comps = groups[group]
        for comp in range(comps.start, comps.start + comps.size):
            for plane in range(planes):
                before, after = in_lines(
                    velocity_z[comp, plane + 1],
                    edge[comp, plane, :, 0:1],
                    edge[comp, plane, :, 1:2],
                )
                sides = (velocity_z[comp, plane] + velocity_z[comp, plane + 2]) + (before + after)
                rest[comp, plane] -= BETA * sides

    send_template(early)
    send_velocity(0, early)
    pl.semaphore_wait(ready_sem, len(mates))
    send_template(apart(others) + within(others))
    send_halo(0)
    send_velocity(1, early)
    send_halo(1)
    last_group = len(groups) - 1

    def by_place(part):
        return [
            (group, some) for some in (part[:1], part[1:]) for group in range(len(groups))
        ]

    def send_from_first():
        for group, part in [
            (0, apart(others)),
            (0, within(front)),
            (last_group, within(front)),
            (last_group, apart(others)),
            *by_place(within(back_rows)),
        ]:
            send_velocity(group, part)

    def send_from_later():
        for group, part in [
            (0, apart(front)),
            (last_group, apart(front)),
            (0, within(others)),
            *by_place(apart(back_rows)),
            (last_group, within(others)),
        ]:
            send_velocity(group, part)

    pl.when(owner == 0)(send_from_first)
    pl.when(owner != 0)(send_from_later)
    for load in loads:
        load.wait()
    arrived(template_y, TEMPLATE)
    transport_lines()
    send_moved()
    moved[:, here_z] = extended[:, column]
    moved_edge[:, here_z] = extended_edge[:, column]
    send_target(early)
    send_target(apart(others) + within(others))
    for group in range(len(groups)):
        velocity_arrived(group)
        beside(group, deliver)
    for group in range(len(groups)):
        to_spectrum(group)
    respond()
    from_spectrum()
    moved_arrived()
    slopes()
    sent(template_y.at[:, pl.ds(0, rows - 1)], TEMPLATE)
    moved_sent()
    for group, comps in enumerate(groups):
        velocity_sent(group)
        beside_arrived(group)
        add_sides(group)
        beside(group, beside_sent)
        if group == 0:
            arrived(target_z, TARGET)
        for comp in range(comps.start, comps.start + comps.size):
            for plane in range(planes):
                misfit = target_z[plane] - moved[plane]
                total = rest[comp, plane] + misfit * slope[comp, plane]
                for tile in range(outer):
                    out[comp, plane, :, tile * LANES : (tile + 1) * LANES] = total[tile]
    target_sent()


def direct(template, target, velocity, departure, weights):
    rows, columns = lax.axis_size("row"), lax.axis_size("col")
    extent_x, _, cells = template.shape
    components = velocity.shape[0]
    planes = extent_x // rows
    lines = rows
    own = lines // columns
    slab = cells // LANES
    outer = slab * columns
    ahead, pairs, back = operators(cells * columns, own)
    tile = (slab, LANES)
    whole = (outer, own, LANES)
    hbm = pl.BlockSpec(memory_space=pl.ANY)
    vmem = pl.BlockSpec(memory_space=pltpu.VMEM)
    kinds = 7 + 5 * 2
    return pl.pallas_call(
        functools.partial(kernel, (rows, columns)),
        out_shape=pltpu.VMEM((components, planes, own, outer * LANES), jnp.float32),
        in_specs=[hbm] * 8,
        out_specs=vmem,
        scratch_shapes=[
            pltpu.VMEM(departure.shape[:2] + tile, jnp.int32),
            pltpu.SMEM(weights.shape[::-1], jnp.float32),
            pltpu.VMEM((planes, lines) + tile, jnp.float32),
            pltpu.VMEM((planes,) + whole, jnp.float32),
            pltpu.VMEM((components, planes + 2) + whole, jnp.float32),
            pltpu.VMEM((components, planes, outer, SUBLANES, LANES), jnp.float32),
            pltpu.VMEM((planes, columns, slab, own, LANES), jnp.float32),
            pltpu.VMEM((planes, columns, slab, SUBLANES, LANES), jnp.float32),
            pltpu.VMEM((planes,) + whole, jnp.float32),
            pltpu.VMEM((planes, outer, SUBLANES, LANES), jnp.float32),
            pltpu.VMEM(whole, jnp.float32),
            pltpu.VMEM(whole, jnp.float32),
            pltpu.VMEM((components, planes) + whole, jnp.float32),
            pltpu.VMEM((components, planes) + whole, jnp.float32),
            pltpu.VMEM((outer, components, planes, own, LANES), jnp.float32),
            pltpu.VMEM(ahead.shape, jnp.bfloat16),
            pltpu.VMEM(pairs.shape, jnp.bfloat16),
            pltpu.VMEM(back.shape, jnp.bfloat16),
            pltpu.SemaphoreType.DMA((5,)),
            pltpu.SemaphoreType.DMA((kinds,)),
            pltpu.SemaphoreType.DMA((kinds,)),
            pltpu.SemaphoreType.REGULAR,
        ],
        compiler_params=pltpu.CompilerParams(collective_id=0, has_side_effects=True),
    )(
        template.reshape((extent_x,) + tile),
        target.reshape((extent_x,) + tile),
        velocity.reshape((components, extent_x) + tile),
        departure.reshape(departure.shape[:2] + tile),
        weights.T,
        jnp.asarray(ahead),
        jnp.asarray(pairs),
        jnp.asarray(back),
    )


def per_block(template, target, velocity, departure, weights):
    rows, columns = lax.axis_size("row"), lax.axis_size("col")
    components = velocity.shape[0]
    one_line = template.shape[1] == 1 and rows % columns == 0 and columns > 1 and components > 1
    whole_tiles = template.shape[2] % (LANES * SUBLANES) == 0
    short = rows // columns == SUBLANES and template.shape[0] % rows == 0
    if one_line and whole_tiles and short:
        return direct(template, target, velocity, departure, weights)
    return per_device(template, target, velocity, departure, weights)


def solution(mesh):
    in_specs = (
        P(None, "row", "col"),
        P(None, "row", "col"),
        P(None, None, "row", "col"),
        P("row", None, "col"),
        P(),
    )
    out_specs = P(None, "row", "col", None)
    return jax.shard_map(
        per_block, mesh=mesh, in_specs=in_specs, out_specs=out_specs, check_vma=False
    )
```

```python
import functools
import math

import jax
import jax.numpy as jnp
import numpy as np
from jax import lax
from jax.experimental import pallas as pl
from jax.experimental.pallas import tpu as pltpu
from jax.sharding import PartitionSpec as P

QUANT = 8
TAPS = 4


BETA = 0.5
HIGH = lax.Precision.HIGHEST
LANES = 128
SUBLANES = 8
MESH = pl.DeviceIdType.MESH


def with_halo(block, sides, width):
    for axis, dim in sides:
        count = lax.axis_size(axis)
        forward = [(i, i + 1) for i in range(count - 1)]
        forward.append((count - 1, 0))
        backward = [(target, source) for source, target in forward]
        low = lax.ppermute(
            lax.slice_in_dim(block, block.shape[dim] - width, None, axis=dim), axis, forward
        )
        high = lax.ppermute(lax.slice_in_dim(block, 0, width, axis=dim), axis, backward)
        block = jnp.concatenate([low, block, high], axis=dim)
    return block


def central(values, axis):
    return (jnp.roll(values, -1, axis) - jnp.roll(values, 1, axis)) * 0.5


def second_difference(values, axis):
    return 2.0 * values - jnp.roll(values, -1, axis) - jnp.roll(values, 1, axis)


def tap_weights(levels, weight):
    taps = []
    for tap in range(TAPS):
        value = jnp.zeros(levels.shape, jnp.float32)
        for level in range(QUANT):
            value = jnp.where(levels == level, weight(level, tap), value)
        taps.append(value)
    return taps


def transport(template_y, departure, weights):
    planes, lines, columns = template_y.shape
    blocks = departure.shape[1]
    span = lines // blocks
    shift_cells = jnp.floor_divide(departure, QUANT)
    levels = departure - shift_cells * QUANT
    taps = tap_weights(levels, lambda level, tap: weights[level, tap])
    shift = jnp.mod(shift_cells + 1, lines)
    parts = []
    for block in range(blocks):
        rolled = template_y
        step = 1
        while step < lines:
            chosen = (shift[:, block : block + 1] & step) != 0
            rolled = jnp.where(chosen, jnp.roll(rolled, step, 1), rolled)
            step *= 2
        part = 0.0
        for tap in range(TAPS):
            turned = jnp.roll(rolled, -tap - block * span, 1)[:, :span]
            part = part + taps[tap][:, block : block + 1] * turned
        parts.append(part)
    return jnp.concatenate(parts, axis=1)


def curvature(velocity_z):
    field_shape = velocity_z.shape
    length = field_shape[-1]
    inner = 128
    outer = length // inner
    lines = velocity_z.reshape(-1, outer, inner)
    angle = 2.0 * math.pi / length
    outer_index = jnp.arange(outer, dtype=jnp.int32)
    inner_index = jnp.arange(inner, dtype=jnp.int32)
    outer_phase = (
        jnp.mod(outer_index[:, None] * outer_index[None, :] * inner, length).astype(jnp.float32)
        * angle
    )
    cos_outer = jnp.cos(outer_phase)
    sin_outer = jnp.sin(outer_phase)
    twist_phase = (
        jnp.mod(outer_index[:, None] * inner_index[None, :], length).astype(jnp.float32) * angle
    )
    cos_twist = jnp.cos(twist_phase)
    sin_twist = jnp.sin(twist_phase)
    inner_phase = (
        jnp.mod(inner_index[:, None] * inner_index[None, :] * outer, length).astype(jnp.float32)
        * angle
    )
    cos_inner = jnp.cos(inner_phase)
    sin_inner = jnp.sin(inner_phase)
    freq_index = outer_index[:, None] + outer * inner_index[None, :]
    signed = jnp.where(freq_index < length // 2, freq_index, freq_index - length).astype(
        jnp.float32
    )
    symbol = (signed * angle) ** 2 / length
    real_one = jnp.einsum("lap,ak->lkp", lines, cos_outer, precision=HIGH)
    imag_one = -jnp.einsum("lap,ak->lkp", lines, sin_outer, precision=HIGH)
    real_two = real_one * cos_twist + imag_one * sin_twist
    imag_two = imag_one * cos_twist - real_one * sin_twist
    real_three = jnp.einsum("lkp,pq->lkq", real_two, cos_inner, precision=HIGH) + jnp.einsum(
        "lkp,pq->lkq", imag_two, sin_inner, precision=HIGH
    )
    imag_three = jnp.einsum("lkp,pq->lkq", imag_two, cos_inner, precision=HIGH) - jnp.einsum(
        "lkp,pq->lkq", real_two, sin_inner, precision=HIGH
    )
    real_three = real_three * symbol
    imag_three = imag_three * symbol
    real_four = jnp.einsum("lkq,pq->lkp", real_three, cos_inner, precision=HIGH) - jnp.einsum(
        "lkq,pq->lkp", imag_three, sin_inner, precision=HIGH
    )
    imag_four = jnp.einsum("lkq,pq->lkp", imag_three, cos_inner, precision=HIGH) + jnp.einsum(
        "lkq,pq->lkp", real_three, sin_inner, precision=HIGH
    )
    real_five = real_four * cos_twist - imag_four * sin_twist
    imag_five = imag_four * cos_twist + real_four * sin_twist
    result = jnp.einsum("lkp,kn->lnp", real_five, cos_outer, precision=HIGH) - jnp.einsum(
        "lkp,kn->lnp", imag_five, sin_outer, precision=HIGH
    )
    return result.reshape(field_shape)


def spectral(arrived):
    return (arrived, curvature(arrived[3:6]))


def per_device(template, target, velocity, departure, weights):
    across = second_difference(velocity, 1)
    bundle = jnp.concatenate([template[None], target[None], velocity, across], axis=0)
    regrouped = lax.all_to_all(bundle, "row", split_axis=1, concat_axis=2, tiled=True)
    moved_image = transport(regrouped[0], departure, weights)
    misfit = regrouped[1] - moved_image
    pull_along = misfit * central(moved_image, 1)
    velocity_y = regrouped[2:5]
    second_part = second_difference(velocity_y, 2)
    second_part = regrouped[5:8] + second_part
    outgoing = jnp.concatenate(
        [misfit[None], moved_image[None], pull_along[None], velocity_y, second_part], axis=0
    )
    columns_z, bending = spectral(
        lax.all_to_all(outgoing, "col", split_axis=2, concat_axis=3, tiled=True)
    )
    misfit_z = columns_z[0]
    moved_z = columns_z[1]
    second_z = columns_z[6:9]
    padded = with_halo(moved_z, (("row", 0),), 1)
    slope_across = (padded[2:] - padded[:-2]) * 0.5
    force = jnp.stack([misfit_z * slope_across, columns_z[2], misfit_z * central(moved_z, 2)])
    return BETA * (second_z + bending) + force


def split_halves(values):
    high = values.astype(jnp.bfloat16)
    return high, (values - high.astype(jnp.float32)).astype(jnp.bfloat16)


def dot_split(left, right):
    dot = functools.partial(jnp.dot, preferred_element_type=jnp.float32)
    return dot(left[0], right[0]) + (dot(left[0], right[1]) + dot(left[1], right[0]))


def halves_of(matrix):
    high = matrix.astype(np.float32).astype(jnp.bfloat16)
    low = (matrix - high.astype(np.float64)).astype(np.float32).astype(jnp.bfloat16)
    return np.stack([high, low])


def operators(length, rows):
    outer = length // LANES
    frequency = np.fft.fftfreq(length) * length
    response = np.real(np.fft.ifft((2.0 * math.pi / length * frequency) ** 2))
    response[0] += 4.0
    response *= BETA
    inner = np.arange(LANES)
    group = np.arange(outer)
    away = np.mod(
        LANES * group[:, None, None] + inner[None, :, None] - inner[None, None, :], length
    )
    mixed = np.fft.fft(response[away], axis=0)
    pairs = []
    forward = np.zeros((outer, outer))
    inverse = np.zeros((outer, outer))
    forward[0] = 1.0
    forward[1] = (-1.0) ** group
    inverse[:, 0] = 1.0 / outer
    inverse[:, 1] = (-1.0) ** group / outer
    zero = np.zeros((LANES, LANES))
    pairs.append(np.block([[mixed[0].real.T, zero], [zero, mixed[outer // 2].real.T]]))
    for k in range(1, outer // 2):
        real, imag = mixed[k].real.T, mixed[k].imag.T
        pairs.append(np.block([[real, imag], [-imag, real]]))
        phase = 2.0 * math.pi * k * group / outer
        forward[2 * k] = np.cos(phase)
        forward[2 * k + 1] = -np.sin(phase)
        inverse[:, 2 * k] = 2.0 * np.cos(phase) / outer
        inverse[:, 2 * k + 1] = -2.0 * np.sin(phase) / outer
    same = np.eye(rows)
    ahead = np.kron(forward, same)
    back = np.kron(inverse, same)
    return halves_of(ahead), halves_of(np.stack(pairs)), halves_of(back)


def kernel(
    extent,
    template,
    target,
    velocity,
    departure_hbm,
    weights_hbm,
    ahead_hbm,
    pairs_hbm,
    back_hbm,
    out,
    departure,
    weights,
    template_y,
    target_z,
    velocity_z,
    edge,
    extended,
    extended_edge,
    moved,
    moved_edge,
    moved_low,
    moved_high,
    slope,
    rest,
    spectrum,
    ahead,
    pairs,
    back,
    load_sem,
    send_sem,
    recv_sem,
    ready_sem,
):
    rows, columns = extent
    row, column = lax.axis_index("row"), lax.axis_index("col")
    planes, lines, slab = template_y.shape[:3]
    components = velocity_z.shape[0]
    own = lines // columns
    outer = columns * slab
    owner = row // own
    place = lax.rem(row, own)
    groups = [pl.ds(0, components - 1), pl.ds(components - 1, 1)]
    TEMPLATE, TARGET, MOVED, MOVED_EDGE, LOW, HIGH_SIDE, VELOCITY = 0, 1, 2, 3, 5, 6, 7
    SIDE_LOW, SIDE_HIGH, EDGE_LOW, EDGE_HIGH = (
        VELOCITY + i * len(groups) for i in range(1, 5)
    )
    extent_x = velocity.shape[1]
    here_z = pl.ds(pl.multiple_of(column * slab, slab), slab)

    loads = [
        pltpu.make_async_copy(source, sink, load_sem.at[i])
        for i, (source, sink) in enumerate(
            [
                (departure_hbm, departure),
                (weights_hbm, weights),
                (ahead_hbm, ahead),
                (pairs_hbm, pairs),
                (back_hbm, back),
            ]
        )
    ]

    near = own // 2
    here = lax.rem(row, near)
    line = [
        (lax.rem(row + i * near, rows), lax.rem(column + j, columns))
        for i in range(rows // near)
        for j in range(columns)
        if i + j > 0
    ]
    mates = [(row - here + lax.rem(here + i, near), column) for i in range(1, near)]
    barrier = pltpu.get_barrier_semaphore()
    for device in line + mates:
        pl.semaphore_signal(barrier, inc=1, device_id=device, device_id_type=MESH)
    for load in loads:
        load.start()
    pl.semaphore_wait(barrier, len(line) + len(mates))
    for device in mates:
        pl.semaphore_signal(ready_sem, inc=1, device_id=device, device_id_type=MESH)

    def remote(source, sink, kind, to):
        return pltpu.make_async_remote_copy(
            src_ref=source,
            dst_ref=sink,
            send_sem=send_sem.at[kind],
            recv_sem=recv_sem.at[kind],
            device_id=to,
            device_id_type=MESH,
        )

    def deliver(source, sink, kind, to, stays=None):
        def go():
            remote(source, sink, kind, to).start()

        if stays is None:
            go()
            return
        pl.when(jnp.logical_not(stays))(go)

        @pl.when(stays)
        def _():
            pltpu.make_async_copy(source, sink, recv_sem.at[kind]).start()

    def sent(ref, kind):
        pltpu.make_async_copy(ref, ref, send_sem.at[kind]).wait()

    def arrived(ref, kind):
        pltpu.make_async_copy(ref, ref, recv_sem.at[kind]).wait()

    inside = owner == column
    def turned(spot):
        return spot // 2 + spot % 2 * (near // 2)

    skipped = here // (near // 2) + here % (near // 2) * 2
    early, front, back_rows = [], [], []
    for d in [*range(1, columns), 0]:
        base = lax.rem(owner + d, columns) * own
        for quad, group in ((0, front), (near, back_rows)):
            if d > 0:
                early.append((False, base + quad + here))
                for k in range(near - 1):
                    after = jnp.where(k >= skipped, turned(k + 1), turned(k))
                    group.append((False, base + quad + after))
            else:
                for k in range(near):
                    group.append((True, base + quad + turned(k)))
    others = front + back_rows

    def apart(rows_of):
        return [(mine, to) for mine, to in rows_of if not mine]

    def within(rows_of):
        return [(mine, to) for mine, to in rows_of if mine]

    def send_template(rows_of):
        for mine, to in rows_of:
            source = template.at[pl.ds(to * planes, planes)]
            sink = template_y.at[:, row]
            deliver(source, sink, TEMPLATE, (to, column), row == to if mine else None)

    def send_target(rows_of):
        for mine, to in rows_of:
            deliver(
                target.at[pl.ds(to * planes, planes)],
                target_z.at[:, here_z, place],
                TARGET,
                (to, owner),
                jnp.logical_and(inside, row == to) if mine else None,
            )

    def send_velocity(group, rows_of):
        comps = groups[group]
        for mine, to in rows_of:
            deliver(
                velocity.at[comps, pl.ds(to * planes, planes)],
                velocity_z.at[comps, pl.ds(1, planes), here_z, place],
                VELOCITY + group,
                (to, owner),
                jnp.logical_and(inside, row == to) if mine else None,
            )

    def send_halo(group):
        comps = groups[group]
        for h in range(columns):
            for to, plane, at in (
                (h * own, (h * own * planes - 1) % extent_x, 0),
                (h * own + own - 1, (h + 1) * own * planes % extent_x, planes + 1),
            ):
                deliver(
                    velocity.at[comps, plane],
                    velocity_z.at[comps, at, here_z, place],
                    VELOCITY + group,
                    (to, owner),
                    jnp.logical_and(inside, row == to),
                )

    def beside(group, go):
        comps = groups[group]
        mine = pl.ds(1, planes)
        @pl.when(place < own - 1)
        def _():
            go(
                velocity_z.at[comps, planes],
                velocity_z.at[comps, 0],
                SIDE_LOW + group,
                (lax.rem(row + 1, rows), column),
            )

        @pl.when(place > 0)
        def _():
            go(
                velocity_z.at[comps, 1],
                velocity_z.at[comps, planes + 1],
                SIDE_HIGH + group,
                (lax.rem(row + rows - 1, rows), column),
            )

        go(
            velocity_z.at[comps, mine, :, own - 1],
            edge.at[comps, :, :, 0],
            EDGE_LOW + group,
            (row, lax.rem(column + 1, columns)),
        )
        go(
            velocity_z.at[comps, mine, :, 0],
            edge.at[comps, :, :, 1],
            EDGE_HIGH + group,
            (row, lax.rem(column + columns - 1, columns)),
        )

    def beside_sent(*copy):
        remote(*copy).wait_send()

    def velocity_sent(group):
        comps = groups[group]
        ends = jnp.logical_or(place == 0, place == own - 1)
        kept = jnp.logical_and(inside, ends)
        total = planes * rows

        @pl.when(inside)
        def _():
            sent(velocity.at[comps, pl.ds(0, total - planes)], VELOCITY + group)

        @pl.when(jnp.logical_not(inside))
        def _():
            sent(velocity.at[comps, pl.ds(0, total)], VELOCITY + group)

        @pl.when(kept)
        def _():
            sent(velocity.at[comps, pl.ds(0, 2 * columns - 1)], VELOCITY + group)

        @pl.when(jnp.logical_not(kept))
        def _():
            sent(velocity.at[comps, pl.ds(0, 2 * columns)], VELOCITY + group)

    def target_sent():
        total = planes * rows

        @pl.when(inside)
        def _():
            sent(target.at[pl.ds(0, total - planes)], TARGET)

        @pl.when(jnp.logical_not(inside))
        def _():
            sent(target.at[pl.ds(0, total)], TARGET)

    def moved_sent():
        for _ in range(columns - 1):
            sent(extended.at[:, 0], MOVED)
            for r in range(2):
                sent(extended_edge.at[:, 0, :, r], MOVED_EDGE + r)
        sent(extended.at[0], LOW)
        sent(extended.at[0], HIGH_SIDE)

    def transport_lines():
        blocks = departure.shape[1]
        span = lines // blocks
        for plane in range(planes):
            image = [template_y[plane, y] for y in range(lines)]
            values = []
            for block in range(blocks):
                offset = departure[plane, block]
                whole = offset >> (QUANT.bit_length() - 1)
                levels = offset - whole * QUANT
                taps = tap_weights(levels, lambda level, tap: weights[tap, level])
                shift = jnp.where(whole + 1 < 0, whole + 1 + lines, whole + 1)
                rolled = image
                step = 1
                while step < lines:
                    chosen = (shift & step) != 0
                    rolled = [
                        jnp.where(chosen, rolled[(y - step) % lines], rolled[y])
                        for y in range(lines)
                    ]
                    step *= 2
                for y in range(block * span, (block + 1) * span):
                    value = taps[0] * rolled[y]
                    for tap in range(1, TAPS):
                        value = value + taps[tap] * rolled[(y + tap) % lines]
                    values.append(value)
            for y in range(lines):
                extended[plane, y // own, :, y % own, :] = values[y]
            for j in range(columns):
                extended_edge[plane, j, :, 0, :] = values[(j * own - 1) % lines]
                extended_edge[plane, j, :, 1, :] = values[(j * own + own) % lines]

    def send_moved():
        up, down = lax.rem(row + 1, rows), lax.rem(row + rows - 1, rows)
        for j in range(columns):
            to = lax.rem(column + j, columns)
            deliver(extended.at[planes - 1, to], moved_low.at[here_z], LOW, (up, to))
            deliver(extended.at[0, to], moved_high.at[here_z], HIGH_SIDE, (down, to))
            if j > 0:
                deliver(extended.at[:, to], moved.at[:, here_z], MOVED, (row, to))
                for r in range(2):
                    deliver(
                        extended_edge.at[:, to, :, r],
                        moved_edge.at[:, here_z, r],
                        MOVED_EDGE + r,
                        (row, to),
                    )
    def velocity_arrived(group):
        comps = groups[group]

        @pl.when(place == 0)
        def _():
            arrived(velocity_z.at[comps, pl.ds(0, planes + 1)], VELOCITY + group)

        @pl.when(place == own - 1)
        def _():
            arrived(velocity_z.at[comps, pl.ds(1, planes + 1)], VELOCITY + group)

        @pl.when(place * (own - 1 - place) > 0)
        def _():
            arrived(velocity_z.at[comps, pl.ds(1, planes)], VELOCITY + group)

    def beside_arrived(group):
        comps = groups[group]
        arrived(edge.at[comps, :, :, 0], EDGE_LOW + group)
        arrived(edge.at[comps, :, :, 1], EDGE_HIGH + group)

        @pl.when(place > 0)
        def _():
            arrived(velocity_z.at[comps, 0], SIDE_LOW + group)

        @pl.when(place < own - 1)
        def _():
            arrived(velocity_z.at[comps, planes + 1], SIDE_HIGH + group)

    def moved_arrived():
        for _ in range(columns - 1):
            arrived(moved.at[:, pl.ds(0, slab)], MOVED)
            for r in range(2):
                arrived(moved_edge.at[:, pl.ds(0, slab), r], MOVED_EDGE + r)
        arrived(moved_low, LOW)
        arrived(moved_high, HIGH_SIDE)

    def in_lines(values, low, high):
        after = jnp.concatenate([values[:, 1:], high], axis=1)
        before = jnp.concatenate([low, values[:, :-1]], axis=1)
        return before, after

    def slopes():
        lane = lax.broadcasted_iota(jnp.int32, (outer, own, LANES), 2)
        for plane in range(planes):
            here = moved[plane]
            below = moved[plane - 1] if plane > 0 else moved_low[...]
            above = moved[plane + 1] if plane < planes - 1 else moved_high[...]
            slope[0, plane] = 0.5 * (above - below)
            before, after = in_lines(
                here, moved_edge[plane, :, 0:1], moved_edge[plane, :, 1:2]
            )
            slope[1, plane] = 0.5 * (after - before)
            following = jnp.roll(here, -1, 2)
            following = jnp.where(lane == LANES - 1, jnp.roll(following, -1, 0), following)
            previous = jnp.roll(here, 1, 2)
            previous = jnp.where(lane == 0, jnp.roll(previous, 1, 0), previous)
            slope[2, plane] = 0.5 * (following - previous)

    def to_spectrum(group):
        ahead_parts = (ahead[0], ahead[1])
        comps = groups[group]
        for comp in range(comps.start, comps.start + comps.size):
            for plane in range(planes):
                block = velocity_z[comp, plane + 1].reshape(outer * own, LANES)
                spectrum[:, comp, plane] = dot_split(ahead_parts, split_halves(block)).reshape(
                    outer, own, LANES
                )

    def respond():
        for pair in range(outer // 2):
            shape = (components * planes * own, LANES)
            joined = jnp.concatenate(
                [spectrum[2 * pair].reshape(shape), spectrum[2 * pair + 1].reshape(shape)], axis=1
            )
            result = dot_split(split_halves(joined), (pairs[0, pair], pairs[1, pair]))
            shape = (components, planes, own, LANES)
            spectrum[2 * pair] = result[:, :LANES].reshape(shape)
            spectrum[2 * pair + 1] = result[:, LANES:].reshape(shape)

    def from_spectrum():
        back_parts = (back[0], back[1])
        for comp in range(components):
            for plane in range(planes):
                block = spectrum[:, comp, plane].reshape(outer * own, LANES)
                result = dot_split(back_parts, split_halves(block))
                rest[comp, plane] = result.reshape(outer, own, LANES)

    def add_sides(comp, plane):
        before, after = in_lines(
            velocity_z[comp, plane + 1],
            edge[comp, plane, :, 0:1],
            edge[comp, plane, :, 1:2],
        )
        sides = (velocity_z[comp, plane] + velocity_z[comp, plane + 2]) + (before + after)
        return rest[comp, plane] - BETA * sides

    send_template(early)
    send_velocity(0, early)
    pl.semaphore_wait(ready_sem, len(mates))
    send_template(apart(others) + within(others))
    send_halo(0)
    send_velocity(1, early)
    send_halo(1)
    last_group = len(groups) - 1

    def by_place(part):
        return [
            (group, some) for some in (part[:1], part[1:]) for group in range(len(groups))
        ]

    def send_from_first():
        for group, part in [
            (0, apart(others)),
            (0, within(front)),
            (last_group, within(front)),
            (last_group, apart(others)),
            *by_place(within(back_rows)),
        ]:
            send_velocity(group, part)

    def send_from_later():
        for group, part in [
            (0, apart(front)),
            (last_group, apart(front)),
            (0, within(others)),
            *by_place(apart(back_rows)),
            (last_group, within(others)),
        ]:
            send_velocity(group, part)

    pl.when(owner == 0)(send_from_first)
    pl.when(owner != 0)(send_from_later)
    for load in loads:
        load.wait()
    arrived(template_y, TEMPLATE)
    transport_lines()
    send_moved()
    moved[:, here_z] = extended[:, column]
    moved_edge[:, here_z] = extended_edge[:, column]
    send_target(apart(back_rows) + apart(front) + within(others))
    send_target(early)
    for group in range(len(groups)):
        velocity_arrived(group)
        beside(group, deliver)
    for group in range(len(groups)):
        to_spectrum(group)
    respond()
    from_spectrum()
    moved_arrived()
    slopes()
    for group, comps in enumerate(groups):
        beside_arrived(group)
        if group == 0:
            arrived(target_z, TARGET)
        for comp in range(comps.start, comps.start + comps.size):
            for plane in range(planes):
                misfit = target_z[plane] - moved[plane]
                total = add_sides(comp, plane) + misfit * slope[comp, plane]
                for tile in range(outer):
                    out[comp, plane, :, tile * LANES : (tile + 1) * LANES] = total[tile]
    sent(template_y.at[:, pl.ds(0, rows - 1)], TEMPLATE)
    moved_sent()
    for group in range(len(groups)):
        velocity_sent(group)
        beside(group, beside_sent)
    target_sent()


def direct(template, target, velocity, departure, weights):
    rows, columns = lax.axis_size("row"), lax.axis_size("col")
    extent_x, _, cells = template.shape
    components = velocity.shape[0]
    planes = extent_x // rows
    lines = rows
    own = lines // columns
    slab = cells // LANES
    outer = slab * columns
    ahead, pairs, back = operators(cells * columns, own)
    tile = (slab, LANES)
    whole = (outer, own, LANES)
    hbm = pl.BlockSpec(memory_space=pl.ANY)
    vmem = pl.BlockSpec(memory_space=pltpu.VMEM)
    kinds = 7 + 5 * 2
    return pl.pallas_call(
        functools.partial(kernel, (rows, columns)),
        out_shape=pltpu.VMEM((components, planes, own, outer * LANES), jnp.float32),
        in_specs=[hbm] * 8,
        out_specs=vmem,
        scratch_shapes=[
            pltpu.VMEM(departure.shape[:2] + tile, jnp.int32),
            pltpu.SMEM(weights.shape[::-1], jnp.float32),
            pltpu.VMEM((planes, lines) + tile, jnp.float32),
            pltpu.VMEM((planes,) + whole, jnp.float32),
            pltpu.VMEM((components, planes + 2) + whole, jnp.float32),
            pltpu.VMEM((components, planes, outer, SUBLANES, LANES), jnp.float32),
            pltpu.VMEM((planes, columns, slab, own, LANES), jnp.float32),
            pltpu.VMEM((planes, columns, slab, SUBLANES, LANES), jnp.float32),
            pltpu.VMEM((planes,) + whole, jnp.float32),
            pltpu.VMEM((planes, outer, SUBLANES, LANES), jnp.float32),
            pltpu.VMEM(whole, jnp.float32),
            pltpu.VMEM(whole, jnp.float32),
            pltpu.VMEM((components, planes) + whole, jnp.float32),
            pltpu.VMEM((components, planes) + whole, jnp.float32),
            pltpu.VMEM((outer, components, planes, own, LANES), jnp.float32),
            pltpu.VMEM(ahead.shape, jnp.bfloat16),
            pltpu.VMEM(pairs.shape, jnp.bfloat16),
            pltpu.VMEM(back.shape, jnp.bfloat16),
            pltpu.SemaphoreType.DMA((5,)),
            pltpu.SemaphoreType.DMA((kinds,)),
            pltpu.SemaphoreType.DMA((kinds,)),
            pltpu.SemaphoreType.REGULAR,
        ],
        compiler_params=pltpu.CompilerParams(collective_id=0, has_side_effects=True),
    )(
        template.reshape((extent_x,) + tile),
        target.reshape((extent_x,) + tile),
        velocity.reshape((components, extent_x) + tile),
        departure.reshape(departure.shape[:2] + tile),
        weights.T,
        jnp.asarray(ahead),
        jnp.asarray(pairs),
        jnp.asarray(back),
    )


def per_block(template, target, velocity, departure, weights):
    rows, columns = lax.axis_size("row"), lax.axis_size("col")
    components = velocity.shape[0]
    one_line = template.shape[1] == 1 and rows % columns == 0 and columns > 1 and components > 1
    whole_tiles = template.shape[2] % (LANES * SUBLANES) == 0
    short = rows // columns == SUBLANES and template.shape[0] % rows == 0
    if one_line and whole_tiles and short:
        return direct(template, target, velocity, departure, weights)
    return per_device(template, target, velocity, departure, weights)


def solution(mesh):
    in_specs = (
        P(None, "row", "col"),
        P(None, "row", "col"),
        P(None, None, "row", "col"),
        P("row", None, "col"),
        P(),
    )
    out_specs = P(None, "row", "col", None)
    return jax.shard_map(
        per_block, mesh=mesh, in_specs=in_specs, out_specs=out_specs, check_vma=False
    )
```

```python
import functools
import math

import jax
import jax.numpy as jnp
import numpy as np
from jax import lax
from jax.experimental import pallas as pl
from jax.experimental.pallas import tpu as pltpu
from jax.sharding import PartitionSpec as P

QUANT = 8
TAPS = 4


BETA = 0.5
HIGH = lax.Precision.HIGHEST
LANES = 128
SUBLANES = 8
MESH = pl.DeviceIdType.MESH


def with_halo(block, sides, width):
    for axis, dim in sides:
        count = lax.axis_size(axis)
        forward = [(i, i + 1) for i in range(count - 1)]
        forward.append((count - 1, 0))
        backward = [(target, source) for source, target in forward]
        low = lax.ppermute(
            lax.slice_in_dim(block, block.shape[dim] - width, None, axis=dim), axis, forward
        )
        high = lax.ppermute(lax.slice_in_dim(block, 0, width, axis=dim), axis, backward)
        block = jnp.concatenate([low, block, high], axis=dim)
    return block


def central(values, axis):
    return (jnp.roll(values, -1, axis) - jnp.roll(values, 1, axis)) * 0.5


def second_difference(values, axis):
    return 2.0 * values - jnp.roll(values, -1, axis) - jnp.roll(values, 1, axis)


def tap_weights(levels, weight):
    taps = []
    for tap in range(TAPS):
        value = jnp.zeros(levels.shape, jnp.float32)
        for level in range(QUANT):
            value = jnp.where(levels == level, weight(level, tap), value)
        taps.append(value)
    return taps


def transport(template_y, departure, weights):
    planes, lines, columns = template_y.shape
    blocks = departure.shape[1]
    span = lines // blocks
    shift_cells = jnp.floor_divide(departure, QUANT)
    levels = departure - shift_cells * QUANT
    taps = tap_weights(levels, lambda level, tap: weights[level, tap])
    shift = jnp.mod(shift_cells + 1, lines)
    parts = []
    for block in range(blocks):
        rolled = template_y
        step = 1
        while step < lines:
            chosen = (shift[:, block : block + 1] & step) != 0
            rolled = jnp.where(chosen, jnp.roll(rolled, step, 1), rolled)
            step *= 2
        part = 0.0
        for tap in range(TAPS):
            turned = jnp.roll(rolled, -tap - block * span, 1)[:, :span]
            part = part + taps[tap][:, block : block + 1] * turned
        parts.append(part)
    return jnp.concatenate(parts, axis=1)


def curvature(velocity_z):
    field_shape = velocity_z.shape
    length = field_shape[-1]
    inner = 128
    outer = length // inner
    lines = velocity_z.reshape(-1, outer, inner)
    angle = 2.0 * math.pi / length
    outer_index = jnp.arange(outer, dtype=jnp.int32)
    inner_index = jnp.arange(inner, dtype=jnp.int32)
    outer_phase = (
        jnp.mod(outer_index[:, None] * outer_index[None, :] * inner, length).astype(jnp.float32)
        * angle
    )
    cos_outer = jnp.cos(outer_phase)
    sin_outer = jnp.sin(outer_phase)
    twist_phase = (
        jnp.mod(outer_index[:, None] * inner_index[None, :], length).astype(jnp.float32) * angle
    )
    cos_twist = jnp.cos(twist_phase)
    sin_twist = jnp.sin(twist_phase)
    inner_phase = (
        jnp.mod(inner_index[:, None] * inner_index[None, :] * outer, length).astype(jnp.float32)
        * angle
    )
    cos_inner = jnp.cos(inner_phase)
    sin_inner = jnp.sin(inner_phase)
    freq_index = outer_index[:, None] + outer * inner_index[None, :]
    signed = jnp.where(freq_index < length // 2, freq_index, freq_index - length).astype(
        jnp.float32
    )
    symbol = (signed * angle) ** 2 / length
    real_one = jnp.einsum("lap,ak->lkp", lines, cos_outer, precision=HIGH)
    imag_one = -jnp.einsum("lap,ak->lkp", lines, sin_outer, precision=HIGH)
    real_two = real_one * cos_twist + imag_one * sin_twist
    imag_two = imag_one * cos_twist - real_one * sin_twist
    real_three = jnp.einsum("lkp,pq->lkq", real_two, cos_inner, precision=HIGH) + jnp.einsum(
        "lkp,pq->lkq", imag_two, sin_inner, precision=HIGH
    )
    imag_three = jnp.einsum("lkp,pq->lkq", imag_two, cos_inner, precision=HIGH) - jnp.einsum(
        "lkp,pq->lkq", real_two, sin_inner, precision=HIGH
    )
    real_three = real_three * symbol
    imag_three = imag_three * symbol
    real_four = jnp.einsum("lkq,pq->lkp", real_three, cos_inner, precision=HIGH) - jnp.einsum(
        "lkq,pq->lkp", imag_three, sin_inner, precision=HIGH
    )
    imag_four = jnp.einsum("lkq,pq->lkp", imag_three, cos_inner, precision=HIGH) + jnp.einsum(
        "lkq,pq->lkp", real_three, sin_inner, precision=HIGH
    )
    real_five = real_four * cos_twist - imag_four * sin_twist
    imag_five = imag_four * cos_twist + real_four * sin_twist
    result = jnp.einsum("lkp,kn->lnp", real_five, cos_outer, precision=HIGH) - jnp.einsum(
        "lkp,kn->lnp", imag_five, sin_outer, precision=HIGH
    )
    return result.reshape(field_shape)


def spectral(arrived):
    return (arrived, curvature(arrived[3:6]))


def per_device(template, target, velocity, departure, weights):
    across = second_difference(velocity, 1)
    bundle = jnp.concatenate([template[None], target[None], velocity, across], axis=0)
    regrouped = lax.all_to_all(bundle, "row", split_axis=1, concat_axis=2, tiled=True)
    moved_image = transport(regrouped[0], departure, weights)
    misfit = regrouped[1] - moved_image
    pull_along = misfit * central(moved_image, 1)
    velocity_y = regrouped[2:5]
    second_part = second_difference(velocity_y, 2)
    second_part = regrouped[5:8] + second_part
    outgoing = jnp.concatenate(
        [misfit[None], moved_image[None], pull_along[None], velocity_y, second_part], axis=0
    )
    columns_z, bending = spectral(
        lax.all_to_all(outgoing, "col", split_axis=2, concat_axis=3, tiled=True)
    )
    misfit_z = columns_z[0]
    moved_z = columns_z[1]
    second_z = columns_z[6:9]
    padded = with_halo(moved_z, (("row", 0),), 1)
    slope_across = (padded[2:] - padded[:-2]) * 0.5
    force = jnp.stack([misfit_z * slope_across, columns_z[2], misfit_z * central(moved_z, 2)])
    return BETA * (second_z + bending) + force


def split_halves(values):
    high = values.astype(jnp.bfloat16)
    return high, (values - high.astype(jnp.float32)).astype(jnp.bfloat16)


def dot_split(left, right):
    dot = functools.partial(jnp.dot, preferred_element_type=jnp.float32)
    return dot(left[0], right[0]) + (dot(left[0], right[1]) + dot(left[1], right[0]))


def halves_of(matrix):
    high = matrix.astype(np.float32).astype(jnp.bfloat16)
    low = (matrix - high.astype(np.float64)).astype(np.float32).astype(jnp.bfloat16)
    return np.stack([high, low])


def operators(length, rows):
    outer = length // LANES
    frequency = np.fft.fftfreq(length) * length
    response = np.real(np.fft.ifft((2.0 * math.pi / length * frequency) ** 2))
    response[0] += 4.0
    response *= BETA
    inner = np.arange(LANES)
    group = np.arange(outer)
    away = np.mod(
        LANES * group[:, None, None] + inner[None, :, None] - inner[None, None, :], length
    )
    mixed = np.fft.fft(response[away], axis=0)
    pairs = []
    forward = np.zeros((outer, outer))
    inverse = np.zeros((outer, outer))
    forward[0] = 1.0
    forward[1] = (-1.0) ** group
    inverse[:, 0] = 1.0 / outer
    inverse[:, 1] = (-1.0) ** group / outer
    zero = np.zeros((LANES, LANES))
    pairs.append(np.block([[mixed[0].real.T, zero], [zero, mixed[outer // 2].real.T]]))
    for k in range(1, outer // 2):
        real, imag = mixed[k].real.T, mixed[k].imag.T
        pairs.append(np.block([[real, imag], [-imag, real]]))
        phase = 2.0 * math.pi * k * group / outer
        forward[2 * k] = np.cos(phase)
        forward[2 * k + 1] = -np.sin(phase)
        inverse[:, 2 * k] = 2.0 * np.cos(phase) / outer
        inverse[:, 2 * k + 1] = -2.0 * np.sin(phase) / outer
    same = np.eye(rows)
    ahead = np.kron(forward, same)
    back = np.kron(inverse, same)
    return halves_of(ahead), halves_of(np.stack(pairs)), halves_of(back)


def kernel(
    extent,
    template,
    target,
    velocity,
    departure_hbm,
    weights_hbm,
    ahead_hbm,
    pairs_hbm,
    back_hbm,
    out,
    departure,
    weights,
    template_y,
    target_z,
    velocity_z,
    edge,
    extended,
    extended_edge,
    moved,
    moved_edge,
    moved_low,
    moved_high,
    slope,
    rest,
    spectrum,
    ahead,
    pairs,
    back,
    load_sem,
    send_sem,
    recv_sem,
    ready_sem,
):
    rows, columns = extent
    row, column = lax.axis_index("row"), lax.axis_index("col")
    planes, lines, slab = template_y.shape[:3]
    components = velocity_z.shape[0]
    own = lines // columns
    outer = columns * slab
    owner = row // own
    place = lax.rem(row, own)
    groups = [pl.ds(0, components - 1), pl.ds(components - 1, 1)]
    TEMPLATE, TARGET, MOVED, MOVED_EDGE, LOW, HIGH_SIDE, VELOCITY = 0, 1, 2, 3, 5, 6, 7
    SIDE_LOW, SIDE_HIGH, EDGE_LOW, EDGE_HIGH = (
        VELOCITY + i * len(groups) for i in range(1, 5)
    )
    extent_x = velocity.shape[1]
    here_z = pl.ds(pl.multiple_of(column * slab, slab), slab)

    loads = [
        pltpu.make_async_copy(source, sink, load_sem.at[i])
        for i, (source, sink) in enumerate(
            [
                (departure_hbm, departure),
                (weights_hbm, weights),
                (ahead_hbm, ahead),
                (pairs_hbm, pairs),
                (back_hbm, back),
            ]
        )
    ]

    near = own // 2
    here = lax.rem(row, near)
    line = [
        (lax.rem(row + i * near, rows), lax.rem(column + j, columns))
        for i in range(rows // near)
        for j in range(columns)
        if i + j > 0
    ]
    mates = [(row - here + lax.rem(here + i, near), column) for i in range(1, near)]
    barrier = pltpu.get_barrier_semaphore()
    for device in line + mates:
        pl.semaphore_signal(barrier, inc=1, device_id=device, device_id_type=MESH)
    for load in loads:
        load.start()
    pl.semaphore_wait(barrier, len(line) + len(mates))
    for device in mates:
        pl.semaphore_signal(ready_sem, inc=1, device_id=device, device_id_type=MESH)

    def remote(source, sink, kind, to):
        return pltpu.make_async_remote_copy(
            src_ref=source,
            dst_ref=sink,
            send_sem=send_sem.at[kind],
            recv_sem=recv_sem.at[kind],
            device_id=to,
            device_id_type=MESH,
        )

    def deliver(source, sink, kind, to, stays=None):
        def go():
            remote(source, sink, kind, to).start()

        if stays is None:
            go()
            return
        pl.when(jnp.logical_not(stays))(go)

        @pl.when(stays)
        def _():
            pltpu.make_async_copy(source, sink, recv_sem.at[kind]).start()

    def sent(ref, kind):
        pltpu.make_async_copy(ref, ref, send_sem.at[kind]).wait()

    def arrived(ref, kind):
        pltpu.make_async_copy(ref, ref, recv_sem.at[kind]).wait()

    inside = owner == column
    def turned(spot):
        return spot // 2 + spot % 2 * (near // 2)

    skipped = here // (near // 2) + here % (near // 2) * 2
    early, front, back_rows = [], [], []
    for d in [*range(1, columns), 0]:
        base = lax.rem(owner + d, columns) * own
        for quad, group in ((0, front), (near, back_rows)):
            if d > 0:
                early.append((False, base + quad + here))
                for k in range(near - 1):
                    after = jnp.where(k >= skipped, turned(k + 1), turned(k))
                    group.append((False, base + quad + after))
            else:
                for k in range(near):
                    group.append((True, base + quad + turned(k)))
    others = front + back_rows

    def apart(rows_of):
        return [(mine, to) for mine, to in rows_of if not mine]

    def within(rows_of):
        return [(mine, to) for mine, to in rows_of if mine]

    def send_template(rows_of):
        for mine, to in rows_of:
            source = template.at[pl.ds(to * planes, planes)]
            sink = template_y.at[:, row]
            deliver(source, sink, TEMPLATE, (to, column), row == to if mine else None)

    def send_target(rows_of):
        for mine, to in rows_of:
            deliver(
                target.at[pl.ds(to * planes, planes)],
                target_z.at[:, here_z, place],
                TARGET,
                (to, owner),
                jnp.logical_and(inside, row == to) if mine else None,
            )

    def send_velocity(group, rows_of):
        comps = groups[group]
        for mine, to in rows_of:
            deliver(
                velocity.at[comps, pl.ds(to * planes, planes)],
                velocity_z.at[comps, pl.ds(1, planes), here_z, place],
                VELOCITY + group,
                (to, owner),
                jnp.logical_and(inside, row == to) if mine else None,
            )

    def send_halo(group):
        comps = groups[group]
        for h in range(columns):
            for to, plane, at in (
                (h * own, (h * own * planes - 1) % extent_x, 0),
                (h * own + own - 1, (h + 1) * own * planes % extent_x, planes + 1),
            ):
                deliver(
                    velocity.at[comps, plane],
                    velocity_z.at[comps, at, here_z, place],
                    VELOCITY + group,
                    (to, owner),
                    jnp.logical_and(inside, row == to),
                )

    def beside(group, go):
        comps = groups[group]
        mine = pl.ds(1, planes)
        @pl.when(place < own - 1)
        def _():
            go(
                velocity_z.at[comps, planes],
                velocity_z.at[comps, 0],
                SIDE_LOW + group,
                (lax.rem(row + 1, rows), column),
            )

        @pl.when(place > 0)
        def _():
            go(
                velocity_z.at[comps, 1],
                velocity_z.at[comps, planes + 1],
                SIDE_HIGH + group,
                (lax.rem(row + rows - 1, rows), column),
            )

        go(
            velocity_z.at[comps, mine, :, own - 1],
            edge.at[comps, :, :, 0],
            EDGE_LOW + group,
            (row, lax.rem(column + 1, columns)),
        )
        go(
            velocity_z.at[comps, mine, :, 0],
            edge.at[comps, :, :, 1],
            EDGE_HIGH + group,
            (row, lax.rem(column + columns - 1, columns)),
        )

    def beside_sent(*copy):
        remote(*copy).wait_send()

    def velocity_sent(group):
        comps = groups[group]
        ends = jnp.logical_or(place == 0, place == own - 1)
        kept = jnp.logical_and(inside, ends)
        total = planes * rows

        @pl.when(inside)
        def _():
            sent(velocity.at[comps, pl.ds(0, total - planes)], VELOCITY + group)

        @pl.when(jnp.logical_not(inside))
        def _():
            sent(velocity.at[comps, pl.ds(0, total)], VELOCITY + group)

        @pl.when(kept)
        def _():
            sent(velocity.at[comps, pl.ds(0, 2 * columns - 1)], VELOCITY + group)

        @pl.when(jnp.logical_not(kept))
        def _():
            sent(velocity.at[comps, pl.ds(0, 2 * columns)], VELOCITY + group)

    def target_sent():
        total = planes * rows

        @pl.when(inside)
        def _():
            sent(target.at[pl.ds(0, total - planes)], TARGET)

        @pl.when(jnp.logical_not(inside))
        def _():
            sent(target.at[pl.ds(0, total)], TARGET)

    def moved_sent():
        for _ in range(columns - 1):
            sent(extended.at[:, 0], MOVED)
            for r in range(2):
                sent(extended_edge.at[:, 0, :, r], MOVED_EDGE + r)
        sent(extended.at[0], LOW)
        sent(extended.at[0], HIGH_SIDE)

    def transport_lines():
        blocks = departure.shape[1]
        span = lines // blocks
        for plane in range(planes):
            image = [template_y[plane, y] for y in range(lines)]
            values = []
            for block in range(blocks):
                offset = departure[plane, block]
                whole = offset >> (QUANT.bit_length() - 1)
                levels = offset - whole * QUANT
                taps = tap_weights(levels, lambda level, tap: weights[tap, level])
                shift = jnp.where(whole + 1 < 0, whole + 1 + lines, whole + 1)
                rolled = image
                step = 1
                while step < lines:
                    chosen = (shift & step) != 0
                    rolled = [
                        jnp.where(chosen, rolled[(y - step) % lines], rolled[y])
                        for y in range(lines)
                    ]
                    step *= 2
                for y in range(block * span, (block + 1) * span):
                    value = taps[0] * rolled[y]
                    for tap in range(1, TAPS):
                        value = value + taps[tap] * rolled[(y + tap) % lines]
                    values.append(value)
            for y in range(lines):
                extended[plane, y // own, :, y % own, :] = values[y]
            for j in range(columns):
                extended_edge[plane, j, :, 0, :] = values[(j * own - 1) % lines]
                extended_edge[plane, j, :, 1, :] = values[(j * own + own) % lines]

    def send_moved():
        up, down = lax.rem(row + 1, rows), lax.rem(row + rows - 1, rows)
        for j in range(columns):
            to = lax.rem(column + j, columns)
            deliver(extended.at[planes - 1, to], moved_low.at[here_z], LOW, (up, to))
            deliver(extended.at[0, to], moved_high.at[here_z], HIGH_SIDE, (down, to))
            if j > 0:
                deliver(extended.at[:, to], moved.at[:, here_z], MOVED, (row, to))
                for r in range(2):
                    deliver(
                        extended_edge.at[:, to, :, r],
                        moved_edge.at[:, here_z, r],
                        MOVED_EDGE + r,
                        (row, to),
                    )
    def velocity_arrived(group):
        comps = groups[group]

        @pl.when(place == 0)
        def _():
            arrived(velocity_z.at[comps, pl.ds(0, planes + 1)], VELOCITY + group)

        @pl.when(place == own - 1)
        def _():
            arrived(velocity_z.at[comps, pl.ds(1, planes + 1)], VELOCITY + group)

        @pl.when(place * (own - 1 - place) > 0)
        def _():
            arrived(velocity_z.at[comps, pl.ds(1, planes)], VELOCITY + group)

    def beside_arrived(group):
        comps = groups[group]
        arrived(edge.at[comps, :, :, 0], EDGE_LOW + group)
        arrived(edge.at[comps, :, :, 1], EDGE_HIGH + group)

        @pl.when(place > 0)
        def _():
            arrived(velocity_z.at[comps, 0], SIDE_LOW + group)

        @pl.when(place < own - 1)
        def _():
            arrived(velocity_z.at[comps, planes + 1], SIDE_HIGH + group)

    def moved_arrived():
        for _ in range(columns - 1):
            arrived(moved.at[:, pl.ds(0, slab)], MOVED)
            for r in range(2):
                arrived(moved_edge.at[:, pl.ds(0, slab), r], MOVED_EDGE + r)
        arrived(moved_low, LOW)
        arrived(moved_high, HIGH_SIDE)

    def in_lines(values, low, high):
        after = jnp.concatenate([values[:, 1:], high], axis=1)
        before = jnp.concatenate([low, values[:, :-1]], axis=1)
        return before, after

    def slopes():
        lane = lax.broadcasted_iota(jnp.int32, (outer, own, LANES), 2)
        for plane in range(planes):
            here = moved[plane]
            below = moved[plane - 1] if plane > 0 else moved_low[...]
            above = moved[plane + 1] if plane < planes - 1 else moved_high[...]
            slope[0, plane] = 0.5 * (above - below)
            before, after = in_lines(
                here, moved_edge[plane, :, 0:1], moved_edge[plane, :, 1:2]
            )
            slope[1, plane] = 0.5 * (after - before)
            following = jnp.roll(here, -1, 2)
            following = jnp.where(lane == LANES - 1, jnp.roll(following, -1, 0), following)
            previous = jnp.roll(here, 1, 2)
            previous = jnp.where(lane == 0, jnp.roll(previous, 1, 0), previous)
            slope[2, plane] = 0.5 * (following - previous)

    def to_spectrum(group):
        ahead_parts = (ahead[0], ahead[1])
        comps = groups[group]
        for comp in range(comps.start, comps.start + comps.size):
            for plane in range(planes):
                block = velocity_z[comp, plane + 1].reshape(outer * own, LANES)
                spectrum[:, comp, plane] = dot_split(ahead_parts, split_halves(block)).reshape(
                    outer, own, LANES
                )

    def respond():
        for pair in range(outer // 2):
            shape = (components * planes * own, LANES)
            joined = jnp.concatenate(
                [spectrum[2 * pair].reshape(shape), spectrum[2 * pair + 1].reshape(shape)], axis=1
            )
            result = dot_split(split_halves(joined), (pairs[0, pair], pairs[1, pair]))
            shape = (components, planes, own, LANES)
            spectrum[2 * pair] = result[:, :LANES].reshape(shape)
            spectrum[2 * pair + 1] = result[:, LANES:].reshape(shape)

    def from_spectrum():
        back_parts = (back[0], back[1])
        for comp in range(components):
            for plane in range(planes):
                block = spectrum[:, comp, plane].reshape(outer * own, LANES)
                result = dot_split(back_parts, split_halves(block))
                rest[comp, plane] = result.reshape(outer, own, LANES)

    def add_sides(comp, plane):
        before, after = in_lines(
            velocity_z[comp, plane + 1],
            edge[comp, plane, :, 0:1],
            edge[comp, plane, :, 1:2],
        )
        sides = (velocity_z[comp, plane] + velocity_z[comp, plane + 2]) + (before + after)
        return rest[comp, plane] - BETA * sides

    last_group = len(groups) - 1
    send_template(early)
    send_velocity(0, early)

    def send_nearest():
        send_velocity(last_group, early[:1])

    pl.when(owner != 0)(send_nearest)
    pl.semaphore_wait(ready_sem, len(mates))
    send_template(apart(others) + within(others))
    send_halo(0)
    pl.when(owner == 0)(send_nearest)
    send_velocity(last_group, early[1:])
    send_halo(1)
    def by_place(part):
        return [
            (group, some) for some in (part[:1], part[1:]) for group in range(len(groups))
        ]

    def send_from_first():
        for group, part in [
            (0, apart(others)),
            (0, within(front)),
            (last_group, within(front)),
            (last_group, apart(others)),
            *by_place(within(back_rows)),
        ]:
            send_velocity(group, part)

    def send_from_later():
        for group, part in [
            (0, apart(front)),
            (last_group, apart(front)),
            (0, within(others)),
            *by_place(apart(back_rows)),
            (last_group, within(others)),
        ]:
            send_velocity(group, part)

    pl.when(owner == 0)(send_from_first)
    pl.when(owner != 0)(send_from_later)
    for load in loads:
        load.wait()
    arrived(template_y, TEMPLATE)
    transport_lines()
    send_moved()
    moved[:, here_z] = extended[:, column]
    moved_edge[:, here_z] = extended_edge[:, column]
    send_target(apart(back_rows) + apart(front) + within(others))
    send_target(early)
    for group in range(len(groups)):
        velocity_arrived(group)
        beside(group, deliver)
    for group in range(len(groups)):
        to_spectrum(group)
    respond()
    from_spectrum()
    moved_arrived()
    slopes()
    for group, comps in enumerate(groups):
        beside_arrived(group)
        if group == 0:
            arrived(target_z, TARGET)
        for comp in range(comps.start, comps.start + comps.size):
            for plane in range(planes):
                misfit = target_z[plane] - moved[plane]
                total = add_sides(comp, plane) + misfit * slope[comp, plane]
                for tile in range(outer):
                    out[comp, plane, :, tile * LANES : (tile + 1) * LANES] = total[tile]
    sent(template_y.at[:, pl.ds(0, rows - 1)], TEMPLATE)
    moved_sent()
    for group in range(len(groups)):
        velocity_sent(group)
        beside(group, beside_sent)
    target_sent()


def direct(template, target, velocity, departure, weights):
    rows, columns = lax.axis_size("row"), lax.axis_size("col")
    extent_x, _, cells = template.shape
    components = velocity.shape[0]
    planes = extent_x // rows
    lines = rows
    own = lines // columns
    slab = cells // LANES
    outer = slab * columns
    ahead, pairs, back = operators(cells * columns, own)
    tile = (slab, LANES)
    whole = (outer, own, LANES)
    hbm = pl.BlockSpec(memory_space=pl.ANY)
    vmem = pl.BlockSpec(memory_space=pltpu.VMEM)
    kinds = 7 + 5 * 2
    return pl.pallas_call(
        functools.partial(kernel, (rows, columns)),
        out_shape=pltpu.VMEM((components, planes, own, outer * LANES), jnp.float32),
        in_specs=[hbm] * 8,
        out_specs=vmem,
        scratch_shapes=[
            pltpu.VMEM(departure.shape[:2] + tile, jnp.int32),
            pltpu.SMEM(weights.shape[::-1], jnp.float32),
            pltpu.VMEM((planes, lines) + tile, jnp.float32),
            pltpu.VMEM((planes,) + whole, jnp.float32),
            pltpu.VMEM((components, planes + 2) + whole, jnp.float32),
            pltpu.VMEM((components, planes, outer, SUBLANES, LANES), jnp.float32),
            pltpu.VMEM((planes, columns, slab, own, LANES), jnp.float32),
            pltpu.VMEM((planes, columns, slab, SUBLANES, LANES), jnp.float32),
            pltpu.VMEM((planes,) + whole, jnp.float32),
            pltpu.VMEM((planes, outer, SUBLANES, LANES), jnp.float32),
            pltpu.VMEM(whole, jnp.float32),
            pltpu.VMEM(whole, jnp.float32),
            pltpu.VMEM((components, planes) + whole, jnp.float32),
            pltpu.VMEM((components, planes) + whole, jnp.float32),
            pltpu.VMEM((outer, components, planes, own, LANES), jnp.float32),
            pltpu.VMEM(ahead.shape, jnp.bfloat16),
            pltpu.VMEM(pairs.shape, jnp.bfloat16),
            pltpu.VMEM(back.shape, jnp.bfloat16),
            pltpu.SemaphoreType.DMA((5,)),
            pltpu.SemaphoreType.DMA((kinds,)),
            pltpu.SemaphoreType.DMA((kinds,)),
            pltpu.SemaphoreType.REGULAR,
        ],
        compiler_params=pltpu.CompilerParams(collective_id=0, has_side_effects=True),
    )(
        template.reshape((extent_x,) + tile),
        target.reshape((extent_x,) + tile),
        velocity.reshape((components, extent_x) + tile),
        departure.reshape(departure.shape[:2] + tile),
        weights.T,
        jnp.asarray(ahead),
        jnp.asarray(pairs),
        jnp.asarray(back),
    )


def per_block(template, target, velocity, departure, weights):
    rows, columns = lax.axis_size("row"), lax.axis_size("col")
    components = velocity.shape[0]
    one_line = template.shape[1] == 1 and rows % columns == 0 and columns > 1 and components > 1
    whole_tiles = template.shape[2] % (LANES * SUBLANES) == 0
    short = rows // columns == SUBLANES and template.shape[0] % rows == 0
    if one_line and whole_tiles and short:
        return direct(template, target, velocity, departure, weights)
    return per_device(template, target, velocity, departure, weights)


def solution(mesh):
    in_specs = (
        P(None, "row", "col"),
        P(None, "row", "col"),
        P(None, None, "row", "col"),
        P("row", None, "col"),
        P(),
    )
    out_specs = P(None, "row", "col", None)
    return jax.shard_map(
        per_block, mesh=mesh, in_specs=in_specs, out_specs=out_specs, check_vma=False
    )
```
